32 devices in a mesh: groups: 2 (over y), ctx: 4 (over z), head: 2 (over x), sub: 2 (over core).
Axes of the slice: x: 2, y: 2, z: 4, core: 2. Of those that a mesh axis runs over, the one named last changes fastest.
Arguments:
- queries: float32 [1024, 32, 128], P(('groups', 'ctx'), ('head', 'sub')), parts along dimension 0, may hold values from -110 to 110
- key_vectors: float32 [1024, 8, 128], P(('groups', 'ctx'), 'head'), parts along dimension 0, may hold values from -110 to 110
- value_vectors: float32 [1024, 8, 128], P(('groups', 'ctx'), 'head'), parts along dimension 0, may hold values from -20 to 20
- query_feature: float32 [32, 128, 128], P(('head', 'sub')), may hold values from -0.5 to 0.5
- key_feature: float32 [32, 128, 128], P(('head', 'sub')), may hold values from -0.5 to 0.5
Outputs:
- query_grad: float32 [1024, 32, 128], P(('groups', 'ctx'), ('head', 'sub')), parts along dimension 0
- key_grad: float32 [1024, 8, 128], P(('groups', 'ctx'), 'head'), parts along dimension 0
- value_grad: float32 [1024, 8, 128], P(('groups', 'ctx'), 'head'), parts along dimension 0
The draws below stay inside these ranges and needn't reach their ends.
There are 2 independent parts, one for each index of `groups`. The reference program is written for one: setup_inputs(seed, part) draws one part's arguments, and reference() takes and returns one part's arrays. A program takes and returns all parts, laid end to end along the dimension named above; an argument that names none is the same for every part. Nothing has to cross between parts.
All inputs are finite; a program needn't handle non-finite values.
Results may differ from the reference program's by a relative error of at most 0.0003.
Values sent between devices are 32-bit elements; how exact they have to be, the bound alone decides.
No kernel may reach another device: no remote copies, remote signals or barrier semaphores. Data moves between devices by JAX's collectives and lax.ppermute only.
A program may use at most 64 MiB of HBM per device.

```python
import math
import jax
import jax.numpy as jnp
from jax import lax

HD = 128
H = 32
KV = 8
BLK = 128
SEQ = 512


def paired_rows(key):
    base = jax.random.fold_in(key, 11)
    parts = jax.random.split(base, 3)
    key_rows = jnp.clip(jax.random.normal(parts[0], (SEQ, KV, HD), jnp.float32), -5.0, 5.0)
    query_rows = jnp.clip(jax.random.normal(parts[2], (SEQ, H, HD), jnp.float32), -5.0, 5.0)
    return (query_rows, key_rows)


def draw_queries(key, part):
    return paired_rows(key)[0]


def draw_key_vectors(key, part):
    return paired_rows(key)[1]


def levels(rng, shape, cuts, smallest, top_value):
    level = 1.0
    for dim, shards_of in cuts:
        heights = jax.random.uniform(jax.random.fold_in(jax.random.fold_in(rng, 6), dim), (shards_of,), jnp.float32, smallest / len(cuts), top_value / len(cuts))
        level = level * jnp.repeat(jnp.exp(heights), shape[dim] // shards_of).reshape((-1,) + (1,) * (len(shape) - 1 - dim))
    return level


def gaussian(own_key, extent, spread, limit, shards=(), kind=jnp.bfloat16):
    gain = levels(own_key, extent, shards, -0.22, 0.18) if shards else 1.0
    entries = jax.random.normal(own_key, extent, jnp.float32) * spread * gain
    return jnp.minimum(jnp.maximum(entries, -limit), limit).astype(kind)


def setup_inputs(seed: int = 0, part: int = 0) -> dict:
    seeds = jax.random.split(jax.random.key(seed), 6)
    part_splits = jax.random.split(jax.random.fold_in(seeds[5], part), 6)
    return {
        "queries": draw_queries(jax.random.fold_in(jax.random.fold_in(seeds[5], part), 71), part),
        "key_vectors": draw_key_vectors(jax.random.fold_in(jax.random.fold_in(seeds[5], part), 71), part),
        "value_vectors": gaussian(part_splits[2], (SEQ, KV, HD), 4.0, 20.0, ((0, 4), (1, 2)), jnp.float32),
        "query_feature": gaussian(seeds[3], (H, HD, HD), HD ** -0.5, 0.5, ((0, 4),), jnp.float32),
        "key_feature": gaussian(seeds[4], (H, HD, HD), HD ** -0.5, 0.5, ((0, 4),), jnp.float32),
    }


neg_large = -1e+30

def feature_map(rows, weight):
    mapped = jnp.dot(rows, weight, precision=lax.Precision.HIGHEST)
    return jnp.concatenate([jax.nn.softmax(mapped, axis=-1), jax.nn.softmax(-mapped, axis=-1)], axis=-1)

def teacher_head(query_rows, key_rows, value_rows):
    score_scale = 1.0 / math.sqrt(HD)
    logit_scores = jnp.dot(query_rows, key_rows.T, precision=lax.Precision.HIGHEST) * score_scale
    position = jnp.arange(SEQ)
    allowed = position[None, :] <= position[:, None]
    probs = jax.nn.softmax(jnp.where(allowed, logit_scores, neg_large), axis=-1)
    return jnp.dot(probs, value_rows, precision=lax.Precision.HIGHEST)

def student_head(query_rows, key_rows, value_rows, query_weight, key_weight):
    count = SEQ // BLK
    score_scale = 1.0 / math.sqrt(HD)
    query_feature_rows = feature_map(query_rows, query_weight).reshape(count, BLK, 2 * HD)
    key_feat = feature_map(key_rows, key_weight).reshape(count, BLK, 2 * HD)
    value_blocks = value_rows.reshape(count, BLK, HD)
    block_states = jnp.einsum('bnf,bnd->bfd', key_feat, value_blocks, precision=lax.Precision.HIGHEST)
    block_norms = lax.optimization_barrier(jnp.sum(key_feat, axis=1))
    running_states = jnp.cumsum(block_states, axis=0)
    running_norms = jnp.cumsum(block_norms, axis=0)
    linear_memory_states = jnp.concatenate([jnp.zeros((2, 2 * HD, HD), jnp.float32), running_states[:-2]], axis=0)
    linear_norms = jnp.concatenate([jnp.zeros((2, 2 * HD), jnp.float32), running_norms[:-2]], axis=0)
    key_blocks = key_rows.reshape(count, BLK, HD)
    shifted_keys = jnp.concatenate([jnp.zeros((1, BLK, HD), jnp.float32), key_blocks[:-1]], axis=0)
    local_window_keys = jnp.concatenate([shifted_keys, key_blocks], axis=1)
    shifted_values = jnp.concatenate([jnp.zeros((1, BLK, HD), jnp.float32), value_blocks[:-1]], axis=0)
    local_window_values = jnp.concatenate([shifted_values, value_blocks], axis=1)
    query_block_list = query_rows.reshape(count, BLK, HD)
    logit_scores = jnp.einsum('lwo,lzo->lwz', query_block_list, local_window_keys, precision=lax.Precision.HIGHEST) * score_scale
    row = jnp.arange(BLK)
    column = jnp.arange(2 * BLK)
    block_ids = jnp.arange(count)
    allowed = jnp.where(column[None, None, :] < BLK, block_ids[:, None, None] > 0, column[None, None, :] - BLK <= row[None, :, None])
    top = lax.stop_gradient(lax.optimization_barrier(jnp.max(jnp.where(allowed, logit_scores, neg_large), axis=-1)))
    softmax_probs = jnp.exp(jnp.where(allowed, logit_scores - top[..., None], neg_large))
    numerator = jnp.einsum('agr,aru->agu', softmax_probs, local_window_values, precision=lax.Precision.HIGHEST)
    numerator = numerator + jnp.einsum('rgk,rkj->rgj', query_feature_rows, linear_memory_states, precision=lax.Precision.HIGHEST)
    denom = lax.optimization_barrier(jnp.sum(softmax_probs, axis=-1)) + jnp.einsum('bqf,bf->bq', query_feature_rows, linear_norms, precision=lax.Precision.HIGHEST)
    return (numerator / denom[..., None]).reshape(SEQ, HD)

def reference(queries, key_vectors, value_vectors, query_feature, key_feature):
    group = H // KV

    def one_teacher(head):
        return teacher_head(queries[:, head], key_vectors[:, head // group], value_vectors[:, head // group])
    target = lax.map(one_teacher, jnp.arange(H, dtype=jnp.int32))

    def loss_of(query_in, key_in, value_in):
        key_rep = jnp.repeat(key_in, group, axis=1)
        value_rep = jnp.repeat(value_in, group, axis=1)
        outputs = jax.vmap(student_head, in_axes=(1, 1, 1, 0, 0))(query_in, key_rep, value_rep, query_feature, key_feature)
        return 0.5 * jnp.sum((outputs - target) ** 2)
    query_grad, key_grad, value_grad = jax.grad(loss_of, argnums=(0, 1, 2))(queries, key_vectors, value_vectors)
    return (query_grad, key_grad, value_grad)
```

```python
import functools
import math

import jax
import jax.numpy as jnp
from jax import lax
from jax.experimental import pallas as pl
from jax.experimental.pallas import tpu as pltpu
from jax.sharding import PartitionSpec as P

NEG = -1e30
F32 = jnp.float32
BF16 = jnp.bfloat16

NT = (((1,), (1,)), ((), ()))
NN = (((1,), (0,)), ((), ()))


def shifted(value, axis, steps):
    count = lax.axis_size(axis)
    first, last = max(0, -steps), min(count, count - steps)
    return lax.ppermute(value, axis, [(i, i + steps) for i in range(first, last)])


def split2(x):
    hi = x.astype(BF16)
    return hi, (x - hi.astype(F32)).astype(BF16)


def split3(x):
    hi = x.astype(BF16)
    rest = x - hi.astype(F32)
    mid = rest.astype(BF16)
    return hi, mid, (rest - mid.astype(F32)).astype(BF16)


def dot(a, b, dims):
    return lax.dot_general(a, b, dims, preferred_element_type=F32)


def mm3(a, b, dims):
    return dot(a[0], b[0], dims) + (dot(a[0], b[1], dims) + dot(a[1], b[0], dims))


def mm6(a, b, dims):
    small = dot(a[0], b[2], dims) + dot(a[2], b[0], dims) + dot(a[1], b[1], dims)
    return dot(a[0], b[0], dims) + (dot(a[0], b[1], dims) + dot(a[1], b[0], dims) + small)


def colsum(x):
    return jnp.sum(x, axis=0, keepdims=True)


def softmax_pair(mapped):
    up = jnp.exp(mapped - jnp.max(mapped, axis=0, keepdims=True))
    low = jnp.exp(jnp.min(mapped, axis=0, keepdims=True) - mapped)
    return up * (1.0 / colsum(up)), low * (1.0 / colsum(low))


def softmax_pair_back(feat, grad, width):
    up, low = feat[:width], feat[width:]
    gup, glow = grad[:width], grad[width:]
    return up * (gup - colsum(up * gup)) - low * (glow - colsum(low * glow))


def pack_kernel(cfg, idx_ref, q_ref, k_ref, v_ref, q4_ref, kv_ref):
    sub = idx_ref[1]
    for g in range(cfg.groups):
        for h in range(cfg.per_group):
            rows = pl.ds(h * cfg.tokens, cfg.tokens)
            q4_ref[g, rows, :] = q_ref[:, g * cfg.per_group + h, :]
        for slot, ref in enumerate((k_ref, v_ref)):
            value = ref[:, cfg.starts[0] + g, :]
            for s in range(1, len(cfg.starts)):
                value = jnp.where(sub == s, ref[:, cfg.starts[s] + g, :], value)
            kv_ref[g, slot] = value


def main_kernel(cfg, idx_ref, q4_ref, own_ref, *refs):
    far_in = refs[: cfg.devices - 1]
    refs = refs[cfg.devices - 1 :]
    wq_ref, wk_ref, dq_ref, down_ref = refs[:4]
    far_out = refs[4 : 4 + cfg.devices - 1]
    (kv_s, dkv_s, fq_s, mx_s, mass_s, tnum_s, num_s, den_s, c_s, fk_s, dfq_s, win_s) = refs[
        4 + cfg.devices - 1 :
    ]
    here = idx_ref[0]
    group = pl.program_id(0)
    tokens, width, per_group = cfg.tokens, cfg.width, cfg.per_group
    rows = per_group * tokens
    scale = 1.0 / math.sqrt(width)

    for k in range(1, cfg.devices):
        kv_s[k] = far_in[k - 1][0]
    kv_s[0] = own_ref[0]

    query = q4_ref[0] * scale
    query_3 = split3(query)
    wk_t = split3(
        jnp.concatenate([wk_ref[h].T for h in range(per_group)], axis=0)
    )

    def head(x, h):
        return x[:, h * tokens : (h + 1) * tokens]

    raw_3 = split3(q4_ref[0])
    for h in range(per_group):
        wq_t = split3(wq_ref[h].T)
        piece = tuple(x[h * tokens : (h + 1) * tokens] for x in raw_3)
        up, low = softmax_pair(mm6(wq_t, piece, NT))
        fq_s[h, :width] = up
        fq_s[h, width:] = low

    key_row = lax.broadcasted_iota(jnp.int32, (tokens, rows), 0)
    query_col = lax.broadcasted_iota(jnp.int32, (tokens, rows), 1) % tokens
    seen = key_row <= query_col
    s_own = jnp.where(seen, mm6(split3(kv_s[0, 0]), query_3, NT), NEG)
    s_prev = jnp.where(here > 0, mm6(split3(kv_s[1, 0]), query_3, NT), NEG)
    top = jnp.maximum(
        jnp.max(s_own, axis=0, keepdims=True), jnp.max(s_prev, axis=0, keepdims=True)
    )
    a_own = jnp.exp(s_own - top)
    a_prev = jnp.exp(s_prev - top)
    mass = colsum(a_own) + colsum(a_prev)
    win_s[0] = a_own
    win_s[1] = a_prev
    wnum = mm3(split2(kv_s[0, 1].T), split2(a_own), NN) + mm3(
        split2(kv_s[1, 1].T), split2(a_prev), NN
    )
    mx_s[...] = top
    mass_s[...] = mass
    tnum_s[...] = wnum
    num_s[...] = wnum
    den_s[...] = mass

    def far_forward(k, carry):
        key, value = kv_s[k, 0], kv_s[k, 1]
        key_3 = split3(key)
        value_t = split2(value.T)
        s = mm6(key_3, query_3, NT)
        old = mx_s[...]
        new = jnp.maximum(old, jnp.max(s, axis=0, keepdims=True))
        p = jnp.exp(s - new)
        factor = jnp.exp(old - new)
        mx_s[...] = new
        mass_s[...] = mass_s[...] * factor + colsum(p)
        tnum_s[...] = tnum_s[...] * factor + mm3(value_t, split2(p), NN)
        mapped = mm6(wk_t, key_3, NT)
        for h in range(per_group):
            up, low = softmax_pair(mapped[h * width : (h + 1) * width])
            fk_t = jnp.concatenate([up, low], axis=0)
            fk_s[k, h] = fk_t
            c_s[k, :, h * tokens : (h + 1) * tokens] = mm3(
                split2(fk_t.T), split2(fq_s[h]), NN
            )
        c = c_s[k]
        num_s[...] += mm3(value_t, split2(c), NN)
        den_s[...] += colsum(c)
        return carry

    lax.fori_loop(2, here + 1, far_forward, 0)

    inv = 1.0 / den_s[...]
    out = num_s[...] * inv
    residual = out - tnum_s[...] * (1.0 / mass_s[...])
    grad = residual * inv
    grad_2 = split2(grad)
    grad_den = -colsum(residual * out) * inv
    query_2 = split2(query)

    dq = jnp.zeros((width, rows), F32)
    for slot in range(2):
        a = win_s[slot]
        soft = a * (mm3(split2(kv_s[slot, 1]), grad_2, NN) + grad_den)
        soft_2 = split2(soft)
        dkv_s[slot, 0] = mm3(soft_2, query_2, NN)
        dkv_s[slot, 1] = mm3(split2(a), grad_2, NT)
        dq = dq + mm3(split2(kv_s[slot, 0].T), soft_2, NN)
    dq = dq * scale

    dfq_s[...] = jnp.zeros_like(dfq_s)
    wk_2 = split2(jnp.concatenate([wk_ref[h] for h in range(per_group)], axis=1))

    def far_backward(k, carry):
        value = kv_s[k, 1]
        dc = mm3(split2(value), grad_2, NN) + grad_den
        dc_2 = split2(dc)
        dkv_s[k, 1] = mm3(split2(c_s[k]), grad_2, NT)
        pieces = []
        for h in range(per_group):
            fk_t = fk_s[k, h]
            dc_h = tuple(head(x, h) for x in dc_2)
            dfq_s[h] += mm3(split2(fk_t), dc_h, NN)
            dfk = mm3(split2(fq_s[h]), dc_h, NT)
            pieces.append(softmax_pair_back(fk_t, dfk, width))
        dkv_s[k, 0] = mm3(wk_2, split2(jnp.concatenate(pieces, axis=0)), NN).T
        return carry

    lax.fori_loop(2, here + 1, far_backward, 0)

    for h in range(per_group):
        back = softmax_pair_back(fq_s[h], dfq_s[h], width)
        dq_h = (head(dq, h) + mm3(split2(wq_ref[h]), split2(back), NN)).T
        for g in range(cfg.groups):

            @pl.when(group == g)
            def _():
                dq_ref[:, g * per_group + h, :] = dq_h

    down_ref[0] = dkv_s[0]
    for k in range(1, cfg.devices):

        @pl.when(here >= k)
        def _():
            far_out[k - 1][0] = dkv_s[k]

        @pl.when(here < k)
        def _():
            far_out[k - 1][0] = jnp.zeros_like(dkv_s[k])


def add_kernel(*refs):
    total = refs[0][...]
    for ref in refs[1:-1]:
        total = total + ref[...]
    refs[-1][...] = total


def place_kernel(cfg, idx_ref, mine_ref, other_ref, dk_ref, dv_ref):
    sub = idx_ref[1]
    for slot, ref in enumerate((dk_ref, dv_ref)):
        for g in range(cfg.groups_dev):
            if cfg.shared:
                ref[:, g, :] = mine_ref[g, slot] + other_ref[g, slot]
            else:
                owner = g // cfg.groups
                local_g = g % cfg.groups
                ref[:, g, :] = jnp.where(
                    sub == owner, mine_ref[local_g, slot], other_ref[local_g, slot]
                )


class Config:
    def __init__(self, queries, key_vectors):
        self.tokens, self.heads, self.width = queries.shape
        self.groups_dev = key_vectors.shape[1]
        self.devices = lax.axis_size("ctx")
        subs = lax.axis_size("sub")
        assert subs == 2
        size = self.heads * subs // self.groups_dev
        self.shared = self.heads < size
        self.groups = max(1, self.heads // size)
        self.per_group = self.heads // self.groups
        self.starts = [s * self.heads // size for s in range(subs)]
        if self.shared:
            assert self.groups_dev == 1


VMEM = pl.BlockSpec(memory_space=pltpu.VMEM)
SMEM = pl.BlockSpec(memory_space=pltpu.SMEM)


def local(queries, key_vectors, value_vectors, query_feature, key_feature):
    cfg = Config(queries, key_vectors)
    tokens, width, groups, per_group = cfg.tokens, cfg.width, cfg.groups, cfg.per_group
    n, rows = cfg.devices, cfg.per_group * cfg.tokens
    idx = jnp.stack([lax.axis_index("ctx"), lax.axis_index("sub")]).astype(jnp.int32)
    kv_shape = jax.ShapeDtypeStruct((groups, 2, tokens, width), F32)
    q4, own = pl.pallas_call(
        functools.partial(pack_kernel, cfg),
        name="pack",
        out_shape=(jax.ShapeDtypeStruct((groups, rows, width), F32), kv_shape),
        in_specs=[SMEM, VMEM, VMEM, VMEM],
        out_specs=(VMEM, VMEM),
    )(idx, queries, key_vectors, value_vectors)
    far = [shifted(own, "ctx", k) for k in range(1, n)]

    kv_spec = pl.BlockSpec((1, 2, tokens, width), lambda g: (g, 0, 0, 0))
    w_spec = pl.BlockSpec((per_group, width, width), lambda g: (g, 0, 0))
    scratch = [
        pltpu.VMEM((n, 2, tokens, width), F32),
        pltpu.VMEM((n, 2, tokens, width), F32),
        pltpu.VMEM((per_group, 2 * width, tokens), F32),
        pltpu.VMEM((1, rows), F32),
        pltpu.VMEM((1, rows), F32),
        pltpu.VMEM((width, rows), F32),
        pltpu.VMEM((width, rows), F32),
        pltpu.VMEM((1, rows), F32),
        pltpu.VMEM((n, tokens, rows), F32),
        pltpu.VMEM((n, per_group, 2 * width, tokens), F32),
        pltpu.VMEM((per_group, 2 * width, tokens), F32),
        pltpu.VMEM((2, tokens, rows), F32),
    ]
    results = pl.pallas_call(
        functools.partial(main_kernel, cfg),
        name="attend",
        grid=(groups,),
        out_shape=(jax.ShapeDtypeStruct(queries.shape, F32), kv_shape) + (kv_shape,) * (n - 1),
        in_specs=[SMEM, pl.BlockSpec((1, rows, width), lambda g: (g, 0, 0)), kv_spec]
        + [kv_spec] * (n - 1)
        + [w_spec, w_spec],
        out_specs=(pl.BlockSpec(queries.shape, lambda g: (0, 0, 0)), kv_spec)
        + (kv_spec,) * (n - 1),
        scratch_shapes=scratch,
        compiler_params=pltpu.CompilerParams(dimension_semantics=("arbitrary",)),
    )(idx, q4, own, *far, query_feature, key_feature)
    query_grad, mine = results[:2]
    back = [shifted(results[1 + k], "ctx", -k) for k in range(1, n)]
    mine = pl.pallas_call(
        add_kernel,
        name="add",
        out_shape=kv_shape,
        in_specs=[VMEM] * n,
        out_specs=VMEM,
    )(mine, *back)
    other = lax.ppermute(mine, "sub", [(0, 1), (1, 0)])
    key_grad, value_grad = pl.pallas_call(
        functools.partial(place_kernel, cfg),
        name="place",
        out_shape=(
            jax.ShapeDtypeStruct(key_vectors.shape, F32),
            jax.ShapeDtypeStruct(value_vectors.shape, F32),
        ),
        in_specs=[SMEM, VMEM, VMEM],
        out_specs=(VMEM, VMEM),
    )(idx, mine, other)
    return query_grad, key_grad, value_grad


def solution(mesh):
    placed = (
        P(("groups", "ctx"), ("head", "sub"), None),
        P(("groups", "ctx"), "head", None),
        P(("groups", "ctx"), "head", None),
        P(("head", "sub"), None, None),
        P(("head", "sub"), None, None),
    )
    return jax.shard_map(
        local,
        mesh=mesh,
        in_specs=placed,
        out_specs=placed[:3],
        check_vma=False,
    )
```

```python
import functools
import math

import jax
import jax.numpy as jnp
from jax import lax
from jax.experimental import pallas as pl
from jax.experimental.pallas import tpu as pltpu
from jax.sharding import PartitionSpec as P

NEG = -1e30
F32 = jnp.float32
BF16 = jnp.bfloat16

NT = (((1,), (1,)), ((), ()))
NN = (((1,), (0,)), ((), ()))


def shifted(value, axis, steps):
    count = lax.axis_size(axis)
    first, last = max(0, -steps), min(count, count - steps)
    return lax.ppermute(value, axis, [(i, i + steps) for i in range(first, last)])


def split2(x):
    hi = x.astype(BF16)
    return hi, (x - hi.astype(F32)).astype(BF16)


def split3(x):
    hi = x.astype(BF16)
    rest = x - hi.astype(F32)
    mid = rest.astype(BF16)
    return hi, mid, (rest - mid.astype(F32)).astype(BF16)


def dot(a, b, dims):
    return lax.dot_general(a, b, dims, preferred_element_type=F32)


def mm3(a, b, dims):
    return dot(a[0], b[0], dims) + (dot(a[0], b[1], dims) + dot(a[1], b[0], dims))


def mm6(a, b, dims):
    small = dot(a[0], b[2], dims) + dot(a[2], b[0], dims) + dot(a[1], b[1], dims)
    return dot(a[0], b[0], dims) + (dot(a[0], b[1], dims) + dot(a[1], b[0], dims) + small)


def colsum(x):
    return jnp.sum(x, axis=0, keepdims=True)


def softmax_pair(mapped):
    up = jnp.exp(mapped - jnp.max(mapped, axis=0, keepdims=True))
    low = jnp.exp(jnp.min(mapped, axis=0, keepdims=True) - mapped)
    return up * (1.0 / colsum(up)), low * (1.0 / colsum(low))


def softmax_pair_back(feat, grad, width):
    up, low = feat[:width], feat[width:]
    gup, glow = grad[:width], grad[width:]
    return up * (gup - colsum(up * gup)) - low * (glow - colsum(low * glow))


def pack_kernel(cfg, k_ref, v_ref, *kv_refs):
    sub = lax.axis_index("sub")
    for g, kv_ref in enumerate(kv_refs):
        for slot, ref in enumerate((k_ref, v_ref)):
            value = ref[:, cfg.starts[0] + g, :]
            for s in range(1, len(cfg.starts)):
                value = jnp.where(sub == s, ref[:, cfg.starts[s] + g, :], value)
            kv_ref[slot] = value


def main_kernel(cfg, group, *refs):
    last = group == cfg.groups - 1
    q_ref, own_ref = refs[:2]
    refs = refs[2:]
    far_in = refs[: cfg.devices - 1]
    refs = refs[cfg.devices - 1 :]
    wq_ref, wk_ref = refs[:2]
    refs = refs[2:]
    dq_in = ()
    if last:
        dq_in = refs[: cfg.groups - 1]
        refs = refs[cfg.groups - 1 :]
    dq_ref, down_ref = refs[:2]
    far_out = refs[2 : 2 + cfg.devices - 1]
    (kv_s, dkv_s, fq_s, mx_s, mass_s, tnum_s, num_s, den_s, c_s, fk_s, dfq_s, win_s) = refs[
        2 + cfg.devices - 1 :
    ]
    here = lax.axis_index("ctx")
    tokens, width, per_group = cfg.tokens, cfg.width, cfg.per_group
    rows = per_group * tokens
    scale = 1.0 / math.sqrt(width)

    for k in range(1, cfg.devices):
        kv_s[k] = far_in[k - 1][...]
    kv_s[0] = own_ref[...]

    raw = jnp.concatenate(
        [q_ref[:, group * per_group + h, :] for h in range(per_group)], axis=0
    )
    query = raw * scale
    query_3 = split3(query)
    wk_t = split3(
        jnp.concatenate([wk_ref[h].T for h in range(per_group)], axis=0)
    )

    def head(x, h):
        return x[:, h * tokens : (h + 1) * tokens]

    raw_3 = split3(raw)
    for h in range(per_group):
        wq_t = split3(wq_ref[h].T)
        piece = tuple(x[h * tokens : (h + 1) * tokens] for x in raw_3)
        up, low = softmax_pair(mm6(wq_t, piece, NT))
        fq_s[h, :width] = up
        fq_s[h, width:] = low

    key_row = lax.broadcasted_iota(jnp.int32, (tokens, rows), 0)
    query_col = lax.broadcasted_iota(jnp.int32, (tokens, rows), 1) % tokens
    seen = key_row <= query_col
    s_own = jnp.where(seen, mm6(split3(kv_s[0, 0]), query_3, NT), NEG)
    s_prev = jnp.where(here > 0, mm6(split3(kv_s[1, 0]), query_3, NT), NEG)
    top = jnp.maximum(
        jnp.max(s_own, axis=0, keepdims=True), jnp.max(s_prev, axis=0, keepdims=True)
    )
    a_own = jnp.exp(s_own - top)
    a_prev = jnp.exp(s_prev - top)
    mass = colsum(a_own) + colsum(a_prev)
    win_s[0] = a_own
    win_s[1] = a_prev
    wnum = mm3(split2(kv_s[0, 1].T), split2(a_own), NN) + mm3(
        split2(kv_s[1, 1].T), split2(a_prev), NN
    )
    mx_s[...] = top
    mass_s[...] = mass
    tnum_s[...] = wnum
    num_s[...] = wnum
    den_s[...] = mass

    def far_forward(k, carry):
        key, value = kv_s[k, 0], kv_s[k, 1]
        key_3 = split3(key)
        value_t = split2(value.T)
        s = mm6(key_3, query_3, NT)
        old = mx_s[...]
        new = jnp.maximum(old, jnp.max(s, axis=0, keepdims=True))
        p = jnp.exp(s - new)
        factor = jnp.exp(old - new)
        mx_s[...] = new
        mass_s[...] = mass_s[...] * factor + colsum(p)
        tnum_s[...] = tnum_s[...] * factor + mm3(value_t, split2(p), NN)
        mapped = mm6(wk_t, key_3, NT)
        for h in range(per_group):
            up, low = softmax_pair(mapped[h * width : (h + 1) * width])
            fk_t = jnp.concatenate([up, low], axis=0)
            fk_s[k, h] = fk_t
            c_s[k, :, h * tokens : (h + 1) * tokens] = mm3(
                split2(fk_t.T), split2(fq_s[h]), NN
            )
        c = c_s[k]
        num_s[...] += mm3(value_t, split2(c), NN)
        den_s[...] += colsum(c)
        return carry

    lax.fori_loop(2, here + 1, far_forward, 0)

    inv = 1.0 / den_s[...]
    out = num_s[...] * inv
    residual = out - tnum_s[...] * (1.0 / mass_s[...])
    grad = residual * inv
    grad_2 = split2(grad)
    grad_den = -colsum(residual * out) * inv
    query_2 = split2(query)

    dq = jnp.zeros((width, rows), F32)
    for slot in range(2):
        a = win_s[slot]
        soft = a * (mm3(split2(kv_s[slot, 1]), grad_2, NN) + grad_den)
        soft_2 = split2(soft)
        dkv_s[slot, 0] = mm3(soft_2, query_2, NN)
        dkv_s[slot, 1] = mm3(split2(a), grad_2, NT)
        dq = dq + mm3(split2(kv_s[slot, 0].T), soft_2, NN)
    dq = dq * scale

    dfq_s[...] = jnp.zeros_like(dfq_s)
    wk_2 = split2(jnp.concatenate([wk_ref[h] for h in range(per_group)], axis=1))

    def far_backward(k, carry):
        value = kv_s[k, 1]
        dc = mm3(split2(value), grad_2, NN) + grad_den
        dc_2 = split2(dc)
        dkv_s[k, 1] = mm3(split2(c_s[k]), grad_2, NT)
        pieces = []
        for h in range(per_group):
            fk_t = fk_s[k, h]
            dc_h = tuple(head(x, h) for x in dc_2)
            dfq_s[h] += mm3(split2(fk_t), dc_h, NN)
            dfk = mm3(split2(fq_s[h]), dc_h, NT)
            pieces.append(softmax_pair_back(fk_t, dfk, width))
        dkv_s[k, 0] = mm3(wk_2, split2(jnp.concatenate(pieces, axis=0)), NN).T
        return carry

    lax.fori_loop(2, here + 1, far_backward, 0)

    for h in range(per_group):
        back = softmax_pair_back(fq_s[h], dfq_s[h], width)
        dq_h = (head(dq, h) + mm3(split2(wq_ref[h]), split2(back), NN)).T
        if last:
            dq_ref[:, group * per_group + h, :] = dq_h
        else:
            dq_ref[h] = dq_h
    for g, ref in enumerate(dq_in):
        for h in range(per_group):
            dq_ref[:, g * per_group + h, :] = ref[h]

    down_ref[...] = dkv_s[0]
    for k in range(1, cfg.devices):

        @pl.when(here >= k)
        def _():
            far_out[k - 1][...] = dkv_s[k]

        @pl.when(here < k)
        def _():
            far_out[k - 1][...] = jnp.zeros_like(dkv_s[k])


def add_kernel(*refs):
    total = refs[0][...]
    for ref in refs[1:-1]:
        total = total + ref[...]
    refs[-1][...] = total


def place_kernel(cfg, *refs):
    sub = lax.axis_index("sub")
    mine, other = refs[: cfg.groups], refs[cfg.groups : 2 * cfg.groups]
    for slot, ref in enumerate(refs[2 * cfg.groups :]):
        for g in range(cfg.groups_dev):
            if cfg.shared:
                ref[:, g, :] = mine[g][slot] + other[g][slot]
            else:
                owner, at = g // cfg.groups, g % cfg.groups
                ref[:, g, :] = jnp.where(sub == owner, mine[at][slot], other[at][slot])


class Config:
    def __init__(self, queries, key_vectors):
        self.tokens, self.heads, self.width = queries.shape
        self.groups_dev = key_vectors.shape[1]
        self.devices = lax.axis_size("ctx")
        subs = lax.axis_size("sub")
        assert subs == 2
        size = self.heads * subs // self.groups_dev
        self.shared = self.heads < size
        self.groups = max(1, self.heads // size)
        self.per_group = self.heads // self.groups
        self.starts = [s * self.heads // size for s in range(subs)]
        if self.shared:
            assert self.groups_dev == 1


VMEM = pl.BlockSpec(memory_space=pltpu.VMEM)
SMEM = pl.BlockSpec(memory_space=pltpu.SMEM)


def local(queries, key_vectors, value_vectors, query_feature, key_feature):
    cfg = Config(queries, key_vectors)
    tokens, width, groups, per_group = cfg.tokens, cfg.width, cfg.groups, cfg.per_group
    n, rows = cfg.devices, cfg.per_group * cfg.tokens
    kv_shape = jax.ShapeDtypeStruct((2, tokens, width), F32)
    own = pl.pallas_call(
        functools.partial(pack_kernel, cfg),
        name="pack",
        out_shape=(kv_shape,) * groups,
        in_specs=[VMEM] * 2,
        out_specs=(VMEM,) * groups,
    )(key_vectors, value_vectors)
    far = [[shifted(own[g], "ctx", k) for k in range(1, n)] for g in range(groups)]

    scratch = [
        pltpu.VMEM((n, 2, tokens, width), F32),
        pltpu.VMEM((n, 2, tokens, width), F32),
        pltpu.VMEM((per_group, 2 * width, tokens), F32),
        pltpu.VMEM((1, rows), F32),
        pltpu.VMEM((1, rows), F32),
        pltpu.VMEM((width, rows), F32),
        pltpu.VMEM((width, rows), F32),
        pltpu.VMEM((1, rows), F32),
        pltpu.VMEM((n, tokens, rows), F32),
        pltpu.VMEM((n, per_group, 2 * width, tokens), F32),
        pltpu.VMEM((per_group, 2 * width, tokens), F32),
        pltpu.VMEM((2, tokens, rows), F32),
    ]
    w_shape = (per_group, width, width)
    dq_parts, mine = [], []
    for g in range(groups):
        last = g == groups - 1
        dq_shape = queries.shape if last else w_shape
        w_spec = pl.BlockSpec(w_shape, lambda i, g=g: (g, 0, 0))
        full = lambda shape: pl.BlockSpec(shape, lambda i: (0,) * len(shape))
        kv_spec = full(kv_shape.shape)
        extra = dq_parts if last else []
        results = pl.pallas_call(
            functools.partial(main_kernel, cfg, g),
            name="attend",
            grid=(1,),
            out_shape=(jax.ShapeDtypeStruct(dq_shape, F32),) + (kv_shape,) * n,
            in_specs=[full(queries.shape)]
            + [kv_spec] * n
            + [w_spec, w_spec]
            + [full(w_shape)] * len(extra),
            out_specs=(full(dq_shape),) + (kv_spec,) * n,
            scratch_shapes=scratch,
        )(queries, own[g], *far[g], query_feature, key_feature, *extra)
        dq_parts.append(results[0])
        back = [shifted(results[1 + k], "ctx", -k) for k in range(1, n)]
        mine.append(
            pl.pallas_call(
                add_kernel,
                name="add",
                out_shape=kv_shape,
                in_specs=[VMEM] * n,
                out_specs=VMEM,
            )(results[1], *back)
        )
    other = [lax.ppermute(part, "sub", [(0, 1), (1, 0)]) for part in mine]
    key_grad, value_grad = pl.pallas_call(
        functools.partial(place_kernel, cfg),
        name="place",
        out_shape=(
            jax.ShapeDtypeStruct(key_vectors.shape, F32),
            jax.ShapeDtypeStruct(value_vectors.shape, F32),
        ),
        in_specs=[VMEM] * (2 * groups),
        out_specs=(VMEM, VMEM),
    )(*mine, *other)
    return dq_parts[-1], key_grad, value_grad


def solution(mesh):
    placed = (
        P(("groups", "ctx"), ("head", "sub"), None),
        P(("groups", "ctx"), "head", None),
        P(("groups", "ctx"), "head", None),
        P(("head", "sub"), None, None),
        P(("head", "sub"), None, None),
    )
    return jax.shard_map(
        local,
        mesh=mesh,
        in_specs=placed,
        out_specs=placed[:3],
        check_vma=False,
    )
```

```python
import functools
import math

import jax
import jax.numpy as jnp
from jax import lax
from jax.experimental import pallas as pl
from jax.experimental.pallas import tpu as pltpu
from jax.sharding import PartitionSpec as P

NEG = -1e30
F32 = jnp.float32
BF16 = jnp.bfloat16

NT = (((1,), (1,)), ((), ()))
NN = (((1,), (0,)), ((), ()))


def shifted(value, axis, steps):
    count = lax.axis_size(axis)
    first, last = max(0, -steps), min(count, count - steps)
    return lax.ppermute(value, axis, [(i, i + steps) for i in range(first, last)])


def split2(x):
    hi = x.astype(BF16)
    return hi, (x - hi.astype(F32)).astype(BF16)


def split3(x):
    hi = x.astype(BF16)
    rest = x - hi.astype(F32)
    mid = rest.astype(BF16)
    return hi, mid, (rest - mid.astype(F32)).astype(BF16)


def lanes(*parts):
    return jnp.concatenate(parts, axis=1)


def stack(*parts):
    return jnp.concatenate(parts, axis=0)


def dot(a, b, dims):
    return lax.dot_general(a, b, dims, preferred_element_type=F32)


def short3(a, b, dims):
    join = lanes if dims is NT else stack
    return dot(lanes(a[0], a[0], a[1]), join(b[0], b[1], b[0]), dims)


def short6(a, b, dims):
    join = lanes if dims is NT else stack
    return dot(
        lanes(a[1], a[2], a[0], a[1], a[0], a[0]),
        join(b[1], b[0], b[2], b[0], b[1], b[0]),
        dims,
    )


def tall3(a, b, dims):
    m = a[0].shape[0]
    both = dot(stack(a[0], a[1]), b[0], dims)
    return both[:m] + (both[m:] + dot(a[0], b[1], dims))


def wide3(a, b, dims):
    if dims is NT:
        n = b[0].shape[0]
        both = dot(a[0], stack(b[0], b[1]), dims)
    else:
        n = b[0].shape[1]
        both = dot(a[0], lanes(b[0], b[1]), dims)
    return both[:, :n] + (both[:, n:] + dot(a[1], b[0], dims))


def colsum(x):
    return jnp.sum(x, axis=0, keepdims=True)


def colmax(x):
    return jnp.max(x, axis=0, keepdims=True)


def softmax_pair(mapped):
    up = jnp.exp(mapped - colmax(mapped))
    low = jnp.exp(jnp.min(mapped, axis=0, keepdims=True) - mapped)
    return stack(up * (1.0 / colsum(up)), low * (1.0 / colsum(low)))


def softmax_pair_back(feat, grad, width):
    up, low = feat[:width], feat[width:]
    gup, glow = grad[:width], grad[width:]
    return up * (gup - colsum(up * gup)) - low * (glow - colsum(low * glow))


def pack_kernel(cfg, k_ref, v_ref, *kv_refs):
    sub = lax.axis_index("sub")
    for g, kv_ref in enumerate(kv_refs):
        for slot, ref in enumerate((k_ref, v_ref)):
            value = ref[:, cfg.starts[0] + g, :]
            for s in range(1, len(cfg.starts)):
                value = jnp.where(sub == s, ref[:, cfg.starts[s] + g, :], value)
            kv_ref[slot] = value


def prep_kernel(cfg, q_ref, wq_ref, wk_ref, *refs):
    own_refs, outs = refs[: cfg.groups], refs[cfg.groups :]
    tokens, width, per_group = cfg.tokens, cfg.width, cfg.per_group
    rows = per_group * tokens
    scale = 1.0 / math.sqrt(width)
    key_row = lax.broadcasted_iota(jnp.int32, (tokens, rows), 0)
    query_col = lax.broadcasted_iota(jnp.int32, (tokens, rows), 1) % tokens
    for g in range(cfg.groups):
        q_out, wk_out, fq_out, a_out, num_out, top_out, mass_out = outs[g::cfg.groups]
        first = g * per_group
        query = split3(stack(*[q_ref[:, first + h, :] for h in range(per_group)]))
        for i in range(3):
            q_out[:, i * width : (i + 1) * width] = query[i]
        scores = short6(split3(own_refs[g][0]), query, NT) * scale
        scores = jnp.where(key_row <= query_col, scores, NEG)
        top = colmax(scores)
        a = jnp.exp(scores - top)
        a_out[...] = a
        top_out[...] = top
        mass_out[...] = colsum(a)
        num_out[...] = short3(split2(own_refs[g][1].T), split2(a), NN)
        for h in range(per_group):
            piece = tuple(x[h * tokens : (h + 1) * tokens] for x in query)
            feat = split2(softmax_pair(short6(split3(wq_ref[first + h].T), piece, NT)))
            fq_out[h, :, :tokens] = feat[0]
            fq_out[h, :, tokens:] = feat[1]
            part = split3(wk_ref[first + h].T)
            for i in range(3):
                wk_out[h * width : (h + 1) * width, i * width : (i + 1) * width] = part[i]


def main_kernel(cfg, group, *refs):
    last = group == cfg.groups - 1
    n = cfg.devices
    q_ref, wk_t_ref, fq_ref, a_ref, num_ref, top_ref, mass_ref, wq_ref, wk_ref = refs[:9]
    kv_in = refs[9 : 9 + n]
    refs = refs[9 + n :]
    dq_in = ()
    if last:
        dq_in = refs[: cfg.groups - 1]
        refs = refs[cfg.groups - 1 :]
    dq_ref = refs[0]
    kv_out = refs[1 : 1 + n]
    (kv_s, dkv_s, top_s, mass_s, tnum_s, num_s, den_s, c_s, fk_s, dfq_s) = refs[1 + n :]
    here = lax.axis_index("ctx")
    tokens, width, per_group = cfg.tokens, cfg.width, cfg.per_group
    rows, feats = per_group * tokens, 2 * width
    pair_rows = 2 * tokens
    scale = 1.0 / math.sqrt(width)

    for k in range(2, n):
        pair, at = k // 2 - 1, (k % 2) * tokens
        for slot in range(2):
            kv_s[pair, slot, at : at + tokens, :] = kv_in[k][slot]
    query = tuple(q_ref[:, i * width : (i + 1) * width] for i in range(3))

    def head(x, h):
        return x[:, h * tokens : (h + 1) * tokens]

    def fq(h):
        return fq_ref[h, :, :tokens], fq_ref[h, :, tokens:]

    key_prev, value_prev = kv_in[1][0], kv_in[1][1]
    s_prev = short6(split3(key_prev), query, NT) * scale
    s_prev = jnp.where(here > 0, s_prev, NEG)
    top = jnp.maximum(top_ref[...], colmax(s_prev))
    a_prev = jnp.exp(s_prev - top)
    fade = jnp.exp(top_ref[...] - top)
    a_own = a_ref[...] * fade
    win_2 = split2(stack(a_own, a_prev))
    mass = mass_ref[...] * fade + colsum(a_prev)
    wnum = num_ref[...] * fade + short3(
        split2(value_prev.T), (win_2[0][tokens:], win_2[1][tokens:]), NN
    )
    top_s[...] = top
    mass_s[...] = mass
    tnum_s[...] = wnum
    num_s[...] = wnum
    den_s[...] = mass

    def far_forward(pair, carry):
        second = here >= 2 * pair + 3
        key, value = kv_s[pair, 0], kv_s[pair, 1]
        key_3 = split3(key)
        s = short6(key_3, query, NT) * scale
        s = stack(s[:tokens], jnp.where(second, s[tokens:], NEG))
        old = top_s[...]
        new = jnp.maximum(old, colmax(s))
        p = jnp.exp(s - new)
        factor = jnp.exp(old - new)
        top_s[...] = new
        mass_s[...] = mass_s[...] * factor + colsum(p)
        wk_t = tuple(wk_t_ref[:, i * width : (i + 1) * width] for i in range(3))
        mapped = short6(wk_t, key_3, NT)
        for h in range(per_group):
            feat_t = softmax_pair(mapped[h * width : (h + 1) * width])
            fk_s[pair, h] = feat_t
            c = wide3(split2(feat_t.T), fq(h), NN)
            c_s[pair, :tokens, h * tokens : (h + 1) * tokens] = c[:tokens]
            c_s[pair, tokens:, h * tokens : (h + 1) * tokens] = jnp.where(
                second, c[tokens:], 0.0
            )
        c = c_s[pair]
        den_s[...] += colsum(c)
        value_t = split2(value.T)
        tnum_s[...] = tnum_s[...] * factor + tall3(value_t, split2(p), NN)
        num_s[...] += tall3(value_t, split2(c), NN)
        return carry

    pairs = here // 2
    lax.fori_loop(0, pairs, far_forward, 0)

    inv = 1.0 / den_s[...]
    out = num_s[...] * inv
    residual = out - tnum_s[...] * (1.0 / mass_s[...])
    grad = residual * inv
    grad_2 = split2(grad)
    grad_den = -colsum(residual * out) * inv
    dfq_s[...] = jnp.zeros_like(dfq_s)

    def far_backward(pair, carry):
        second = here >= 2 * pair + 3
        dc = short3(split2(kv_s[pair, 1]), grad_2, NN) + grad_den
        dc = stack(dc[:tokens], jnp.where(second, dc[tokens:], 0.0))
        dc_2 = split2(dc)
        dkv_s[pair, 1] = wide3(split2(c_s[pair]), grad_2, NT)
        pieces = []
        for h in range(per_group):
            feat_t = fk_s[pair, h]
            dc_h = tuple(head(x, h) for x in dc_2)
            dfq_s[h] += wide3(split2(feat_t), dc_h, NN)
            dfk = short3(fq(h), dc_h, NT)
            pieces.append(softmax_pair_back(feat_t, dfk, width))
        wk_2 = split2(lanes(*[wk_ref[h] for h in range(per_group)]))
        dkv_s[pair, 0] = tall3(wk_2, split2(stack(*pieces)), NN).T
        return carry

    lax.fori_loop(0, pairs, far_backward, 0)
    for k in range(2, n):
        pair, at = k // 2 - 1, (k % 2) * tokens

        @pl.when(here >= k)
        def _():
            for slot in range(2):
                kv_out[k][slot] = dkv_s[pair, slot, at : at + tokens, :]

        @pl.when(here < k)
        def _():
            kv_out[k][...] = jnp.zeros((2, tokens, width), F32)

    key_win = stack(kv_in[0][0], key_prev)
    value_win = stack(kv_in[0][1], value_prev)
    soft = short3(split2(value_win), grad_2, NN) + grad_den
    soft = stack(a_own, a_prev) * soft * scale
    soft_2 = split2(soft)
    dk = wide3(soft_2, query[:2], NN)
    dv = wide3(win_2, grad_2, NT)
    for k in range(2):
        kv_out[k][0] = dk[k * tokens : (k + 1) * tokens]
        kv_out[k][1] = dv[k * tokens : (k + 1) * tokens]
    dq = tall3(split2(key_win.T), soft_2, NN)
    for h in range(per_group):
        feat = fq(h)
        feat = feat[0].astype(F32) + feat[1].astype(F32)
        back = softmax_pair_back(feat, dfq_s[h], width)
        dq_h = (head(dq, h) + short3(split2(wq_ref[h]), split2(back), NN)).T
        if last:
            dq_ref[:, group * per_group + h, :] = dq_h
        else:
            dq_ref[h] = dq_h
    for g, ref in enumerate(dq_in):
        for h in range(per_group):
            dq_ref[:, g * per_group + h, :] = ref[h]


def add_kernel(*refs):
    total = refs[0][...]
    for ref in refs[1:-1]:
        total = total + ref[...]
    refs[-1][...] = total


def place_kernel(cfg, *refs):
    sub = lax.axis_index("sub")
    mine, other = refs[: cfg.groups], refs[cfg.groups : 2 * cfg.groups]
    for slot, ref in enumerate(refs[2 * cfg.groups :]):
        for g in range(cfg.groups_dev):
            if cfg.shared:
                ref[:, g, :] = mine[g][slot] + other[g][slot]
            else:
                owner, at = g // cfg.groups, g % cfg.groups
                ref[:, g, :] = jnp.where(sub == owner, mine[at][slot], other[at][slot])


class Config:
    def __init__(self, queries, key_vectors):
        self.tokens, self.heads, self.width = queries.shape
        self.groups_dev = key_vectors.shape[1]
        self.devices = lax.axis_size("ctx")
        subs = lax.axis_size("sub")
        assert subs == 2
        size = self.heads * subs // self.groups_dev
        self.shared = self.heads < size
        self.groups = max(1, self.heads // size)
        self.per_group = self.heads // self.groups
        self.starts = [s * self.heads // size for s in range(subs)]
        if self.shared:
            assert self.groups_dev == 1


VMEM = pl.BlockSpec(memory_space=pltpu.VMEM)


def limit(mebibytes):
    return pltpu.CompilerParams(vmem_limit_bytes=mebibytes << 20)


def near(*arrays):
    return [pltpu.with_memory_space_constraint(x, pltpu.VMEM) for x in arrays]


def local(queries, key_vectors, value_vectors, query_feature, key_feature):
    cfg = Config(queries, key_vectors)
    tokens, width, groups, per_group = cfg.tokens, cfg.width, cfg.groups, cfg.per_group
    n, rows = cfg.devices, cfg.per_group * cfg.tokens
    pairs = max(1, (n - 1) // 2)
    kv_shape = pltpu.VMEM((2, tokens, width), F32)
    own = pl.pallas_call(
        functools.partial(pack_kernel, cfg),
        name="pack",
        out_shape=(kv_shape,) * groups,
        in_specs=[VMEM] * 2,
        out_specs=(VMEM,) * groups,
        compiler_params=limit(8),
    )(key_vectors, value_vectors)
    far = [[shifted(own[g], "ctx", k) for k in range(1, n)] for g in range(groups)]

    prep_shapes = (
        pltpu.VMEM((rows, 3 * width), BF16),
        pltpu.VMEM((per_group * width, 3 * width), BF16),
        pltpu.VMEM((per_group, 2 * width, 2 * tokens), BF16),
        pltpu.VMEM((tokens, rows), F32),
        pltpu.VMEM((width, rows), F32),
        pltpu.VMEM((1, rows), F32),
        pltpu.VMEM((1, rows), F32),
    )
    prep = pl.pallas_call(
        functools.partial(prep_kernel, cfg),
        name="prep",
        out_shape=tuple(shape for shape in prep_shapes for _ in range(groups)),
        in_specs=[VMEM] * (3 + groups),
        out_specs=(VMEM,) * (len(prep_shapes) * groups),
        compiler_params=limit(24),
    )(queries, query_feature, key_feature, *near(*own))

    scratch = [
        pltpu.VMEM((pairs, 2, 2 * tokens, width), F32),
        pltpu.VMEM((pairs, 2, 2 * tokens, width), F32),
        pltpu.VMEM((1, rows), F32),
        pltpu.VMEM((1, rows), F32),
        pltpu.VMEM((width, rows), F32),
        pltpu.VMEM((width, rows), F32),
        pltpu.VMEM((1, rows), F32),
        pltpu.VMEM((pairs, 2 * tokens, rows), F32),
        pltpu.VMEM((pairs, per_group, 2 * width, 2 * tokens), F32),
        pltpu.VMEM((per_group, 2 * width, tokens), F32),
    ]
    w_shape = (per_group, width, width)
    dq_parts, mine = [], []
    for g in range(groups):
        last = g == groups - 1
        dq_shape = jax.ShapeDtypeStruct(queries.shape, F32) if last else pltpu.VMEM(w_shape, F32)
        w_spec = pl.BlockSpec(w_shape, lambda i, g=g: (g, 0, 0))
        extra = dq_parts if last else []
        results = pl.pallas_call(
            functools.partial(main_kernel, cfg, g),
            name="attend",
            grid=(1,),
            out_shape=(dq_shape,) + (kv_shape,) * n,
            in_specs=[VMEM] * len(prep_shapes)
            + [w_spec, w_spec]
            + [VMEM] * (n + len(extra)),
            out_specs=(VMEM,) * (n + 1),
            scratch_shapes=scratch,
            compiler_params=limit(24),
        )(
            *near(*prep[g::groups]),
            query_feature,
            key_feature,
            *near(own[g], *far[g], *extra),
        )
        dq_parts.append(results[0])
        back = [shifted(results[1 + k], "ctx", -k) for k in range(1, n)]
        mine.append(
            pl.pallas_call(
                add_kernel,
                name="add",
                out_shape=kv_shape,
                in_specs=[VMEM] * n,
                out_specs=VMEM,
                compiler_params=limit(8),
            )(*near(results[1], *back))
        )
    other = [lax.ppermute(part, "sub", [(0, 1), (1, 0)]) for part in mine]
    key_grad, value_grad = pl.pallas_call(
        functools.partial(place_kernel, cfg),
        name="place",
        out_shape=(
            jax.ShapeDtypeStruct(key_vectors.shape, F32),
            jax.ShapeDtypeStruct(value_vectors.shape, F32),
        ),
        in_specs=[VMEM] * (2 * groups),
        out_specs=(VMEM, VMEM),
        compiler_params=limit(8),
    )(*near(*mine, *other))
    return dq_parts[-1], key_grad, value_grad


def solution(mesh):
    placed = (
        P(("groups", "ctx"), ("head", "sub"), None),
        P(("groups", "ctx"), "head", None),
        P(("groups", "ctx"), "head", None),
        P(("head", "sub"), None, None),
        P(("head", "sub"), None, None),
    )
    return jax.shard_map(
        local,
        mesh=mesh,
        in_specs=placed,
        out_specs=placed[:3],
        check_vma=False,
    )
```

```python
import functools
import math

import jax
import jax.numpy as jnp
from jax import lax
from jax.experimental import pallas as pl
from jax.experimental.pallas import tpu as pltpu
from jax.sharding import PartitionSpec as P


NEG = -1e30
F32 = jnp.float32
BF16 = jnp.bfloat16

NT = (((1,), (1,)), ((), ()))
NN = (((1,), (0,)), ((), ()))


def shifted(value, axis, steps):
    count = lax.axis_size(axis)
    first, last = max(0, -steps), min(count, count - steps)
    return lax.ppermute(value, axis, [(i, i + steps) for i in range(first, last)])


def split2(x):
    hi = x.astype(BF16)
    return hi, (x - hi.astype(F32)).astype(BF16)


def split3(x):
    hi = x.astype(BF16)
    rest = x - hi.astype(F32)
    mid = rest.astype(BF16)
    return hi, mid, (rest - mid.astype(F32)).astype(BF16)


def lanes(*parts):
    return jnp.concatenate(parts, axis=1)


def stack(*parts):
    return jnp.concatenate(parts, axis=0)


def dot(a, b, dims):
    return lax.dot_general(a, b, dims, preferred_element_type=F32)


def short3(a, b, dims):
    join = lanes if dims is NT else stack
    return dot(lanes(a[0], a[0], a[1]), join(b[0], b[1], b[0]), dims)


def short6(a, b, dims):
    join = lanes if dims is NT else stack
    return dot(
        lanes(a[1], a[2], a[0], a[1], a[0], a[0]),
        join(b[1], b[0], b[2], b[0], b[1], b[0]),
        dims,
    )


def tall3(a, b, dims):
    m = a[0].shape[0]
    both = dot(stack(a[0], a[1]), b[0], dims)
    return both[:m] + (both[m:] + dot(a[0], b[1], dims))


def wide3(a, b, dims):
    if dims is NT:
        n = b[0].shape[0]
        both = dot(a[0], stack(b[0], b[1]), dims)
    else:
        n = b[0].shape[1]
        both = dot(a[0], lanes(b[0], b[1]), dims)
    return both[:, :n] + (both[:, n:] + dot(a[1], b[0], dims))


def colsum(x):
    return jnp.sum(x, axis=0, keepdims=True)


def colmax(x):
    return jnp.max(x, axis=0, keepdims=True)


def softmax_pair(mapped):
    up = jnp.exp(mapped - colmax(mapped))
    low = jnp.exp(jnp.min(mapped, axis=0, keepdims=True) - mapped)
    return stack(up * (1.0 / colsum(up)), low * (1.0 / colsum(low)))


def softmax_pair_back(feat, grad, width):
    up, low = feat[:width], feat[width:]
    gup, glow = grad[:width], grad[width:]
    return up * (gup - colsum(up * gup)) - low * (glow - colsum(low * glow))


def pack_kernel(cfg, k_hbm, v_hbm, *refs):
    kv_refs, (k_ref, v_ref, sems) = refs[: cfg.groups], refs[cfg.groups :]
    copies = [
        pltpu.make_async_copy(src, dst, sems.at[i])
        for i, (src, dst) in enumerate(((k_hbm, k_ref), (v_hbm, v_ref)))
    ]
    for copy in copies:
        copy.start()
    sub = lax.axis_index("sub")
    for slot, ref in enumerate((k_ref, v_ref)):
        copies[slot].wait()
        for g, kv_ref in enumerate(kv_refs):
            value = ref[:, cfg.starts[0] + g, :]
            for s in range(1, len(cfg.starts)):
                value = jnp.where(sub == s, ref[:, cfg.starts[s] + g, :], value)
            kv_ref[slot] = value


def prep_kernel(cfg, q_ref, wq_ref, wk_ref, *refs):
    own_refs, outs = refs[: cfg.groups], refs[cfg.groups :]
    tokens, width, per_group = cfg.tokens, cfg.width, cfg.per_group
    rows = per_group * tokens
    scale = 1.0 / math.sqrt(width)
    key_row = lax.broadcasted_iota(jnp.int32, (tokens, rows), 0)
    query_col = lax.broadcasted_iota(jnp.int32, (tokens, rows), 1) % tokens
    for g in range(cfg.groups):
        (
            q_out, wk_out, fq_out, wk2_out, wq2_out, a_out, num_out, top_out, mass_out
        ) = outs[g::cfg.groups]
        first = g * per_group
        query = split3(stack(*[q_ref[:, first + h, :] for h in range(per_group)]))
        for i in range(3):
            q_out[:, i * width : (i + 1) * width] = query[i]
        scores = short6(split3(own_refs[g][0]), query, NT) * scale
        scores = jnp.where(key_row <= query_col, scores, NEG)
        top = colmax(scores)
        a = jnp.exp(scores - top)
        a_out[...] = a
        top_out[...] = top
        mass_out[...] = colsum(a)
        num_out[...] = short3(split2(own_refs[g][1].T), split2(a), NN)
        for h in range(per_group):
            piece = tuple(x[h * tokens : (h + 1) * tokens] for x in query)
            feat = split2(softmax_pair(short6(split3(wq_ref[first + h].T), piece, NT)))
            fq_out[h, :, :tokens] = feat[0]
            fq_out[h, :, tokens:] = feat[1]
            part = split3(wk_ref[first + h].T)
            for i in range(3):
                wk_out[h * width : (h + 1) * width, i * width : (i + 1) * width] = part[i]
            for out, part in (
                (wk2_out, split2(wk_ref[first + h])),
                (wq2_out, split2(wq_ref[first + h])),
            ):
                for i in range(2):
                    at = i * per_group + h
                    out[:, at * width : (at + 1) * width] = part[i]


def attend_kernel(cfg, *refs):
    n = cfg.devices
    q_ref, wk_t_ref, fq_ref, wk2_ref, a_ref, num_ref, top_ref, mass_ref = refs[:8]
    kv_in = (None,) + refs[8 : 7 + n]
    win_ref, grad_ref, gden_ref, dfq_s = refs[7 + n : 11 + n]
    kv_out = (None, None) + refs[11 + n : 9 + 2 * n]
    (kv_s, dkv_s, top_s, mass_s, tnum_s, num_s, den_s, c_s, fk_s) = refs[9 + 2 * n :]
    here = lax.axis_index("ctx")
    tokens, width, per_group = cfg.tokens, cfg.width, cfg.per_group
    scale = 1.0 / math.sqrt(width)

    for k in range(2, n):
        pair, at = k // 2 - 1, (k % 2) * tokens
        for slot in range(2):
            kv_s[pair, slot, at : at + tokens, :] = kv_in[k][slot]
    query = tuple(q_ref[:, i * width : (i + 1) * width] for i in range(3))

    def head(x, h):
        return x[:, h * tokens : (h + 1) * tokens]

    def fq(h):
        return fq_ref[h, :, :tokens], fq_ref[h, :, tokens:]

    key_prev, value_prev = kv_in[1][0], kv_in[1][1]
    s_prev = short6(split3(key_prev), query, NT) * scale
    s_prev = jnp.where(here > 0, s_prev, NEG)
    top = jnp.maximum(top_ref[...], colmax(s_prev))
    a_prev = jnp.exp(s_prev - top)
    fade = jnp.exp(top_ref[...] - top)
    a_own = a_ref[...] * fade
    win_ref[:tokens] = a_own
    win_ref[tokens:] = a_prev
    mass = mass_ref[...] * fade + colsum(a_prev)
    wnum = num_ref[...] * fade + short3(
        split2(value_prev.T), split2(a_prev), NN
    )
    top_s[...] = top
    mass_s[...] = mass
    tnum_s[...] = wnum
    num_s[...] = wnum
    den_s[...] = mass

    def far_forward(pair, carry):
        second = here >= 2 * pair + 3
        key, value = kv_s[pair, 0], kv_s[pair, 1]
        key_3 = split3(key)
        s = short6(key_3, query, NT) * scale
        s = stack(s[:tokens], jnp.where(second, s[tokens:], NEG))
        old = top_s[...]
        new = jnp.maximum(old, colmax(s))
        p = jnp.exp(s - new)
        factor = jnp.exp(old - new)
        top_s[...] = new
        mass_s[...] = mass_s[...] * factor + colsum(p)
        wk_t = tuple(wk_t_ref[:, i * width : (i + 1) * width] for i in range(3))
        mapped = short6(wk_t, key_3, NT)
        for h in range(per_group):
            feat_t = softmax_pair(mapped[h * width : (h + 1) * width])
            fk_s[pair, h] = feat_t
            c = wide3(split2(feat_t.T), fq(h), NN)
            c_s[pair, :tokens, h * tokens : (h + 1) * tokens] = c[:tokens]
            c_s[pair, tokens:, h * tokens : (h + 1) * tokens] = jnp.where(
                second, c[tokens:], 0.0
            )
        c = c_s[pair]
        den_s[...] += colsum(c)
        value_t = split2(value.T)
        tnum_s[...] = tnum_s[...] * factor + tall3(value_t, split2(p), NN)
        num_s[...] += tall3(value_t, split2(c), NN)
        return carry

    pairs = here // 2
    lax.fori_loop(0, pairs, far_forward, 0)

    inv = 1.0 / den_s[...]
    out = num_s[...] * inv
    residual = out - tnum_s[...] * (1.0 / mass_s[...])
    grad = residual * inv
    grad_2 = split2(grad)
    grad_ref[0] = grad_2[0]
    grad_ref[1] = grad_2[1]
    grad_den = -colsum(residual * out) * inv
    gden_ref[...] = grad_den
    dfq_s[...] = jnp.zeros_like(dfq_s)

    def far_backward(pair, carry):
        second = here >= 2 * pair + 3
        dc = short3(split2(kv_s[pair, 1]), grad_2, NN) + grad_den
        dc = stack(dc[:tokens], jnp.where(second, dc[tokens:], 0.0))
        dc_2 = split2(dc)
        dkv_s[pair, 1] = wide3(split2(c_s[pair]), grad_2, NT)
        pieces = []
        for h in range(per_group):
            feat_t = fk_s[pair, h]
            dc_h = tuple(head(x, h) for x in dc_2)
            dfq_s[h] += wide3(split2(feat_t), dc_h, NN)
            dfk = short3(fq(h), dc_h, NT)
            pieces.append(softmax_pair_back(feat_t, dfk, width))
        wk_2 = wk2_ref[:, : per_group * width], wk2_ref[:, per_group * width :]
        dkv_s[pair, 0] = tall3(wk_2, split2(stack(*pieces)), NN).T
        return carry

    lax.fori_loop(0, pairs, far_backward, 0)
    for k in range(2, n):
        pair, at = k // 2 - 1, (k % 2) * tokens

        @pl.when(here >= k)
        def _():
            for slot in range(2):
                kv_out[k][slot] = dkv_s[pair, slot, at : at + tokens, :]

        @pl.when(here < k)
        def _():
            kv_out[k][...] = jnp.zeros((2, tokens, width), F32)


def window_kernel(cfg, *refs):
    q_ref, win_ref, grad_ref, gden_ref, own_ref, prev_ref, soft_ref = refs[:7]
    outs = refs[7:]
    tokens, width = cfg.tokens, cfg.width
    scale = 1.0 / math.sqrt(width)
    grad_2 = grad_ref[0], grad_ref[1]
    win = win_ref[...]
    soft = short3(split2(stack(own_ref[1], prev_ref[1])), grad_2, NN) + gden_ref[...]
    soft_2 = split2(win * soft * scale)
    soft_ref[0] = soft_2[0]
    soft_ref[1] = soft_2[1]
    dk = wide3(soft_2, (q_ref[:, :width], q_ref[:, width : 2 * width]), NN)
    dv = wide3(split2(win), grad_2, NT)
    for k, out in enumerate(outs):
        out[0] = dk[k * tokens : (k + 1) * tokens]
        out[1] = dv[k * tokens : (k + 1) * tokens]


def query_kernel(cfg, *refs):
    dq_ref = refs[-1]
    tokens, width, per_group = cfg.tokens, cfg.width, cfg.per_group
    for g in range(cfg.groups):
        soft_ref, dfq_ref, fq_ref, wq2_ref, own_ref, prev_ref = refs[:-1][g :: cfg.groups]
        key_t = split2(stack(own_ref[0], prev_ref[0]).T)
        dq = tall3(key_t, (soft_ref[0], soft_ref[1]), NN)
        for h in range(per_group):
            feat = fq_ref[h, :, :tokens].astype(F32) + fq_ref[h, :, tokens:].astype(F32)
            back = softmax_pair_back(feat, dfq_ref[h], width)
            wq_2 = tuple(
                wq2_ref[:, (i * per_group + h) * width : (i * per_group + h + 1) * width]
                for i in range(2)
            )
            dq_h = dq[:, h * tokens : (h + 1) * tokens] + short3(wq_2, split2(back), NN)
            dq_ref[:, g * per_group + h, :] = dq_h.T


def add_kernel(*refs):
    total = refs[0][...]
    for ref in refs[1:-1]:
        total = total + ref[...]
    refs[-1][...] = total


def place_kernel(cfg, *refs):
    sub = lax.axis_index("sub")
    mine, other = refs[: cfg.groups], refs[cfg.groups : 2 * cfg.groups]
    for slot, ref in enumerate(refs[2 * cfg.groups :]):
        for g in range(cfg.groups_dev):
            if cfg.shared:
                ref[:, g, :] = mine[g][slot] + other[g][slot]
            else:
                owner, at = g // cfg.groups, g % cfg.groups
                ref[:, g, :] = jnp.where(sub == owner, mine[at][slot], other[at][slot])


class Config:
    def __init__(self, queries, key_vectors):
        self.tokens, self.heads, self.width = queries.shape
        self.groups_dev = key_vectors.shape[1]
        self.devices = lax.axis_size("ctx")
        subs = lax.axis_size("sub")
        assert subs == 2
        size = self.heads * subs // self.groups_dev
        self.shared = self.heads < size
        self.groups = max(1, self.heads // size)
        self.per_group = self.heads // self.groups
        self.starts = [s * self.heads // size for s in range(subs)]
        if self.shared:
            assert self.groups_dev == 1


VMEM = pl.BlockSpec(memory_space=pltpu.VMEM)


def limit(mebibytes):
    return pltpu.CompilerParams(vmem_limit_bytes=mebibytes << 20)


def near(*arrays):
    return [pltpu.with_memory_space_constraint(x, pltpu.VMEM) for x in arrays]


def call(kernel, outs, args, scratch=(), ins=None, megabytes=16):
    return pl.pallas_call(
        kernel,
        out_shape=outs,
        in_specs=ins or [VMEM] * len(args),
        out_specs=jax.tree.map(lambda _: VMEM, outs),
        scratch_shapes=scratch,
        compiler_params=limit(megabytes),
    )(*args)


def layer(queries, key_vectors, value_vectors, query_feature, key_feature):
    cfg = Config(queries, key_vectors)
    tokens, width, groups, per_group = cfg.tokens, cfg.width, cfg.groups, cfg.per_group
    n, rows = cfg.devices, cfg.per_group * cfg.tokens
    pairs = max(1, (n - 1) // 2)
    kv_shape = pltpu.VMEM((2, tokens, width), F32)
    own = call(
        functools.partial(pack_kernel, cfg),
        (kv_shape,) * groups,
        (key_vectors, value_vectors),
        [
            pltpu.VMEM(key_vectors.shape, F32),
            pltpu.VMEM(value_vectors.shape, F32),
            pltpu.SemaphoreType.DMA((2,)),
        ],
        [pl.BlockSpec(memory_space=pltpu.HBM)] * 2,
    )
    kv = []
    for g in range(groups):
        kv.append([own[g]])
        for k in range(1, n):
            kv[g].append(shifted(own[g], "ctx", k))

    prep_shapes = (
        pltpu.VMEM((rows, 3 * width), BF16),
        pltpu.VMEM((per_group * width, 3 * width), BF16),
        pltpu.VMEM((per_group, 2 * width, 2 * tokens), BF16),
        pltpu.VMEM((width, 2 * per_group * width), BF16),
        pltpu.VMEM((width, 2 * per_group * width), BF16),
        pltpu.VMEM((tokens, rows), F32),
        pltpu.VMEM((width, rows), F32),
        pltpu.VMEM((1, rows), F32),
        pltpu.VMEM((1, rows), F32),
    )
    prep = call(
        functools.partial(prep_kernel, cfg),
        tuple(shape for shape in prep_shapes for _ in range(groups)),
        (queries, query_feature, key_feature, *near(*own)),
    )
    attend_shapes = (
        pltpu.VMEM((2 * tokens, rows), F32),
        pltpu.VMEM((2, width, rows), BF16),
        pltpu.VMEM((1, rows), F32),
        pltpu.VMEM((per_group, 2 * width, tokens), F32),
    )
    scratch = [
        pltpu.VMEM((pairs, 2, 2 * tokens, width), F32),
        pltpu.VMEM((pairs, 2, 2 * tokens, width), F32),
        pltpu.VMEM((1, rows), F32),
        pltpu.VMEM((1, rows), F32),
        pltpu.VMEM((width, rows), F32),
        pltpu.VMEM((width, rows), F32),
        pltpu.VMEM((1, rows), F32),
        pltpu.VMEM((pairs, 2 * tokens, rows), F32),
        pltpu.VMEM((pairs, per_group, 2 * width, 2 * tokens), F32),
    ]
    for_query, mine = [], []
    for g in range(groups):
        q_3, wk_t, fq, wk_2, wq_2, *window = prep[g::groups]
        win, grad, gden, dfq, *grads = call(
            functools.partial(attend_kernel, cfg),
            attend_shapes + (kv_shape,) * (n - 2),
            near(q_3, wk_t, fq, wk_2, *window, *kv[g][1:]),
            scratch,
            megabytes=20,
        )
        soft, *near_grads = call(
            functools.partial(window_kernel, cfg),
            (pltpu.VMEM((2, 2 * tokens, rows), BF16), kv_shape, kv_shape),
            near(q_3, win, grad, gden, kv[g][0], kv[g][1]),
        )
        grads = near_grads + grads
        for_query.append((soft, dfq, fq, wq_2, kv[g][0], kv[g][1]))
        back = []
        for k in range(1, n):
            back.append(shifted(grads[k], "ctx", -k))
        mine.append(call(add_kernel, kv_shape, near(grads[0], *back)))
    query_grad = call(
        functools.partial(query_kernel, cfg),
        jax.ShapeDtypeStruct(queries.shape, F32),
        near(*[x for parts in zip(*for_query) for x in parts]),
    )
    other = [lax.ppermute(part, "sub", [(0, 1), (1, 0)]) for part in mine]
    key_grad, value_grad = call(
        functools.partial(place_kernel, cfg),
        (
            jax.ShapeDtypeStruct(key_vectors.shape, F32),
            jax.ShapeDtypeStruct(value_vectors.shape, F32),
        ),
        near(*mine, *other),
    )
    return query_grad, key_grad, value_grad


def solution(mesh):
    placed = (
        P(("groups", "ctx"), ("head", "sub"), None),
        P(("groups", "ctx"), "head", None),
        P(("groups", "ctx"), "head", None),
        P(("head", "sub"), None, None),
        P(("head", "sub"), None, None),
    )

    def step(queries, key_vectors, value_vectors, query_feature, key_feature):
        return jax.shard_map(
            layer,
            mesh=mesh,
            in_specs=placed,
            out_specs=placed[:3],
            check_vma=False,
        )(queries, key_vectors, value_vectors, query_feature, key_feature)

    return step
```

```python
import functools
import math

import jax
import jax.numpy as jnp
from jax import lax
from jax.experimental import pallas as pl
from jax.experimental.pallas import tpu as pltpu
from jax.sharding import PartitionSpec as P


NEG = -1e30
F32 = jnp.float32
BF16 = jnp.bfloat16

NT = (((1,), (1,)), ((), ()))
NN = (((1,), (0,)), ((), ()))


def shifted(value, axis, steps):
    count = lax.axis_size(axis)
    first, last = max(0, -steps), min(count, count - steps)
    return lax.ppermute(value, axis, [(i, i + steps) for i in range(first, last)])


def split2(x):
    hi = x.astype(BF16)
    return hi, (x - hi.astype(F32)).astype(BF16)


def split3(x):
    hi = x.astype(BF16)
    rest = x - hi.astype(F32)
    mid = rest.astype(BF16)
    return hi, mid, (rest - mid.astype(F32)).astype(BF16)


def lanes(*parts):
    return jnp.concatenate(parts, axis=1)


def stack(*parts):
    return jnp.concatenate(parts, axis=0)


def dot(a, b, dims):
    return lax.dot_general(a, b, dims, preferred_element_type=F32)


def short3(a, b, dims):
    join = lanes if dims is NT else stack
    return dot(lanes(a[0], a[0], a[1]), join(b[0], b[1], b[0]), dims)


def short6(a, b, dims):
    join = lanes if dims is NT else stack
    return dot(
        lanes(a[1], a[2], a[0], a[1], a[0], a[0]),
        join(b[1], b[0], b[2], b[0], b[1], b[0]),
        dims,
    )


def tall3(a, b, dims):
    m = a[0].shape[0]
    both = dot(stack(a[0], a[1]), b[0], dims)
    return both[:m] + (both[m:] + dot(a[0], b[1], dims))


def wide3(a, b, dims):
    if dims is NT:
        n = b[0].shape[0]
        both = dot(a[0], stack(b[0], b[1]), dims)
    else:
        n = b[0].shape[1]
        both = dot(a[0], lanes(b[0], b[1]), dims)
    return both[:, :n] + (both[:, n:] + dot(a[1], b[0], dims))


def colsum(x):
    return jnp.sum(x, axis=0, keepdims=True)


def colmax(x):
    return jnp.max(x, axis=0, keepdims=True)


def softmax_pair(mapped):
    up = jnp.exp(mapped - colmax(mapped))
    low = jnp.exp(jnp.min(mapped, axis=0, keepdims=True) - mapped)
    return stack(up * (1.0 / colsum(up)), low * (1.0 / colsum(low)))


def softmax_pair_back(feat, grad, width):
    up, low = feat[:width], feat[width:]
    gup, glow = grad[:width], grad[width:]
    return up * (gup - colsum(up * gup)) - low * (glow - colsum(low * glow))


def pack_kernel(cfg, k_hbm, v_hbm, *refs):
    kv_refs, (k_ref, v_ref, sems) = refs[: cfg.groups], refs[cfg.groups :]
    copies = [
        pltpu.make_async_copy(src, dst, sems.at[i])
        for i, (src, dst) in enumerate(((k_hbm, k_ref), (v_hbm, v_ref)))
    ]
    for copy in copies:
        copy.start()
    sub = lax.axis_index("sub")
    for slot, ref in enumerate((k_ref, v_ref)):
        copies[slot].wait()
        for g, kv_ref in enumerate(kv_refs):
            value = ref[:, cfg.starts[0] + g, :]
            for s in range(1, len(cfg.starts)):
                value = jnp.where(sub == s, ref[:, cfg.starts[s] + g, :], value)
            kv_ref[slot] = value


def prep_kernel(cfg, *refs):
    sources, own_refs, outs = refs[:3], refs[3 : 3 + cfg.groups], refs[3 + cfg.groups : -4]
    q_ref, wq_ref, wk_ref, sems = refs[-4:]
    copies = [
        pltpu.make_async_copy(src, dst, sems.at[i])
        for i, (src, dst) in enumerate(zip(sources, (q_ref, wq_ref, wk_ref)))
    ]
    for copy in copies:
        copy.start()
    for copy in copies:
        copy.wait()
    tokens, width, per_group = cfg.tokens, cfg.width, cfg.per_group
    rows = per_group * tokens
    scale = 1.0 / math.sqrt(width)
    key_row = lax.broadcasted_iota(jnp.int32, (tokens, rows), 0)
    query_col = lax.broadcasted_iota(jnp.int32, (tokens, rows), 1) % tokens
    for g in range(cfg.groups):
        (
            q_out, wk_out, fq_out, wk2_out, wq2_out, a_out, num_out, top_out, mass_out
        ) = outs[g::cfg.groups]
        first = g * per_group
        query = split3(stack(*[q_ref[:, first + h, :] for h in range(per_group)]))
        for i in range(3):
            q_out[:, i * width : (i + 1) * width] = query[i]
        scores = short6(split3(own_refs[g][0]), query, NT) * scale
        scores = jnp.where(key_row <= query_col, scores, NEG)
        top = colmax(scores)
        a = jnp.exp(scores - top)
        a_out[...] = a
        top_out[...] = top
        mass_out[...] = colsum(a)
        num_out[...] = short3(split2(own_refs[g][1].T), split2(a), NN)
        for h in range(per_group):
            piece = tuple(x[h * tokens : (h + 1) * tokens] for x in query)
            feat = split2(softmax_pair(short6(split3(wq_ref[first + h].T), piece, NT)))
            fq_out[h, :, :tokens] = feat[0]
            fq_out[h, :, tokens:] = feat[1]
            part = split3(wk_ref[first + h].T)
            for i in range(3):
                wk_out[h * width : (h + 1) * width, i * width : (i + 1) * width] = part[i]
            for out, part in (
                (wk2_out, split2(wk_ref[first + h])),
                (wq2_out, split2(wq_ref[first + h])),
            ):
                for i in range(2):
                    at = i * per_group + h
                    out[:, at * width : (at + 1) * width] = part[i]


def attend_kernel(cfg, *refs):
    n = cfg.devices
    q_ref, wk_t_ref, fq_ref, wk2_ref, a_ref, num_ref, top_ref, mass_ref = refs[:8]
    kv_in = (None,) + refs[8 : 7 + n]
    win_ref, grad_ref, gden_ref, dfq_s = refs[7 + n : 11 + n]
    kv_out = (None, None) + refs[11 + n : 9 + 2 * n]
    (kv_s, dkv_s, top_s, mass_s, tnum_s, num_s, den_s, c_s, fk_s) = refs[9 + 2 * n :]
    here = lax.axis_index("ctx")
    tokens, width, per_group = cfg.tokens, cfg.width, cfg.per_group
    scale = 1.0 / math.sqrt(width)

    for k in range(2, n):
        pair, at = k // 2 - 1, (k % 2) * tokens
        for slot in range(2):
            kv_s[pair, slot, at : at + tokens, :] = kv_in[k][slot]
    query = tuple(q_ref[:, i * width : (i + 1) * width] for i in range(3))

    def head(x, h):
        return x[:, h * tokens : (h + 1) * tokens]

    def fq(h):
        return fq_ref[h, :, :tokens], fq_ref[h, :, tokens:]

    key_prev, value_prev = kv_in[1][0], kv_in[1][1]
    s_prev = short6(split3(key_prev), query, NT) * scale
    s_prev = jnp.where(here > 0, s_prev, NEG)
    top = jnp.maximum(top_ref[...], colmax(s_prev))
    a_prev = jnp.exp(s_prev - top)
    fade = jnp.exp(top_ref[...] - top)
    a_own = a_ref[...] * fade
    win_ref[:tokens] = a_own
    win_ref[tokens:] = a_prev
    mass = mass_ref[...] * fade + colsum(a_prev)
    wnum = num_ref[...] * fade + short3(
        split2(value_prev.T), split2(a_prev), NN
    )
    top_s[...] = top
    mass_s[...] = mass
    tnum_s[...] = wnum
    num_s[...] = wnum
    den_s[...] = mass

    def far_forward(pair, carry):
        second = here >= 2 * pair + 3
        key, value = kv_s[pair, 0], kv_s[pair, 1]
        key_3 = split3(key)
        s = short6(key_3, query, NT) * scale
        s = stack(s[:tokens], jnp.where(second, s[tokens:], NEG))
        old = top_s[...]
        new = jnp.maximum(old, colmax(s))
        p = jnp.exp(s - new)
        factor = jnp.exp(old - new)
        top_s[...] = new
        mass_s[...] = mass_s[...] * factor + colsum(p)
        wk_t = tuple(wk_t_ref[:, i * width : (i + 1) * width] for i in range(3))
        mapped = short6(wk_t, key_3, NT)
        for h in range(per_group):
            feat_t = softmax_pair(mapped[h * width : (h + 1) * width])
            fk_s[pair, h] = feat_t
            c = wide3(split2(feat_t.T), fq(h), NN)
            c_s[pair, :tokens, h * tokens : (h + 1) * tokens] = c[:tokens]
            c_s[pair, tokens:, h * tokens : (h + 1) * tokens] = jnp.where(
                second, c[tokens:], 0.0
            )
        c = c_s[pair]
        den_s[...] += colsum(c)
        value_t = split2(value.T)
        tnum_s[...] = tnum_s[...] * factor + tall3(value_t, split2(p), NN)
        num_s[...] += tall3(value_t, split2(c), NN)
        return carry

    pairs = here // 2
    lax.fori_loop(0, pairs, far_forward, 0)

    inv = 1.0 / den_s[...]
    out = num_s[...] * inv
    residual = out - tnum_s[...] * (1.0 / mass_s[...])
    grad = residual * inv
    grad_2 = split2(grad)
    grad_ref[0] = grad_2[0]
    grad_ref[1] = grad_2[1]
    grad_den = -colsum(residual * out) * inv
    gden_ref[...] = grad_den
    dfq_s[...] = jnp.zeros_like(dfq_s)

    def far_backward(pair, carry):
        second = here >= 2 * pair + 3
        dc = short3(split2(kv_s[pair, 1]), grad_2, NN) + grad_den
        dc = stack(dc[:tokens], jnp.where(second, dc[tokens:], 0.0))
        dc_2 = split2(dc)
        dkv_s[pair, 1] = wide3(split2(c_s[pair]), grad_2, NT)
        pieces = []
        for h in range(per_group):
            feat_t = fk_s[pair, h]
            dc_h = tuple(head(x, h) for x in dc_2)
            dfq_s[h] += wide3(split2(feat_t), dc_h, NN)
            dfk = short3(fq(h), dc_h, NT)
            pieces.append(softmax_pair_back(feat_t, dfk, width))
        wk_2 = wk2_ref[:, : per_group * width], wk2_ref[:, per_group * width :]
        dkv_s[pair, 0] = tall3(wk_2, split2(stack(*pieces)), NN).T
        return carry

    lax.fori_loop(0, pairs, far_backward, 0)
    for k in range(2, n):
        pair, at = k // 2 - 1, (k % 2) * tokens

        @pl.when(here >= k)
        def _():
            for slot in range(2):
                kv_out[k][slot] = dkv_s[pair, slot, at : at + tokens, :]

        @pl.when(here < k)
        def _():
            kv_out[k][...] = jnp.zeros((2, tokens, width), F32)


def window_kernel(cfg, *refs):
    q_ref, win_ref, grad_ref, gden_ref, own_ref, prev_ref, soft_ref = refs[:7]
    outs = refs[7:]
    tokens, width = cfg.tokens, cfg.width
    scale = 1.0 / math.sqrt(width)
    grad_2 = grad_ref[0], grad_ref[1]
    win = win_ref[...]
    soft = short3(split2(stack(own_ref[1], prev_ref[1])), grad_2, NN) + gden_ref[...]
    soft_2 = split2(win * soft * scale)
    soft_ref[0] = soft_2[0]
    soft_ref[1] = soft_2[1]
    dk = wide3(soft_2, (q_ref[:, :width], q_ref[:, width : 2 * width]), NN)
    dv = wide3(split2(win), grad_2, NT)
    for k, out in enumerate(outs):
        out[0] = dk[k * tokens : (k + 1) * tokens]
        out[1] = dv[k * tokens : (k + 1) * tokens]


def query_kernel(cfg, *refs):
    dq_ref = refs[-1]
    tokens, width, per_group = cfg.tokens, cfg.width, cfg.per_group
    for g in range(cfg.groups):
        soft_ref, dfq_ref, fq_ref, wq2_ref, own_ref, prev_ref = refs[:-1][g :: cfg.groups]
        key_t = split2(stack(own_ref[0], prev_ref[0]).T)
        dq = tall3(key_t, (soft_ref[0], soft_ref[1]), NN)
        for h in range(per_group):
            feat = fq_ref[h, :, :tokens].astype(F32) + fq_ref[h, :, tokens:].astype(F32)
            back = softmax_pair_back(feat, dfq_ref[h], width)
            wq_2 = tuple(
                wq2_ref[:, (i * per_group + h) * width : (i * per_group + h + 1) * width]
                for i in range(2)
            )
            dq_h = dq[:, h * tokens : (h + 1) * tokens] + short3(wq_2, split2(back), NN)
            dq_ref[:, g * per_group + h, :] = dq_h.T


def add_kernel(*refs):
    total = refs[0][...]
    for ref in refs[1:-1]:
        total = total + ref[...]
    refs[-1][...] = total


def place_kernel(cfg, *refs):
    sub = lax.axis_index("sub")
    mine, other = refs[: cfg.groups], refs[cfg.groups : 2 * cfg.groups]
    for slot, ref in enumerate(refs[2 * cfg.groups :]):
        for g in range(cfg.groups_dev):
            if cfg.shared:
                ref[:, g, :] = mine[g][slot] + other[g][slot]
            else:
                owner, at = g // cfg.groups, g % cfg.groups
                ref[:, g, :] = jnp.where(sub == owner, mine[at][slot], other[at][slot])


class Config:
    def __init__(self, queries, key_vectors):
        self.tokens, self.heads, self.width = queries.shape
        self.groups_dev = key_vectors.shape[1]
        self.devices = lax.axis_size("ctx")
        subs = lax.axis_size("sub")
        assert subs == 2
        size = self.heads * subs // self.groups_dev
        self.shared = self.heads < size
        self.groups = max(1, self.heads // size)
        self.per_group = self.heads // self.groups
        self.starts = [s * self.heads // size for s in range(subs)]
        if self.shared:
            assert self.groups_dev == 1


VMEM = pl.BlockSpec(memory_space=pltpu.VMEM)


def limit(mebibytes):
    return pltpu.CompilerParams(vmem_limit_bytes=mebibytes << 20)


def near(*arrays):
    return [pltpu.with_memory_space_constraint(x, pltpu.VMEM) for x in arrays]


def far_off(*arrays):
    return [pltpu.with_memory_space_constraint(x, pltpu.HBM) for x in arrays]


def call(kernel, outs, args, scratch=(), ins=None, megabytes=16):
    return pl.pallas_call(
        kernel,
        out_shape=outs,
        in_specs=ins or [VMEM] * len(args),
        out_specs=jax.tree.map(lambda _: VMEM, outs),
        scratch_shapes=scratch,
        compiler_params=limit(megabytes),
    )(*args)


def layer(queries, key_vectors, value_vectors, query_feature, key_feature):
    cfg = Config(queries, key_vectors)
    tokens, width, groups, per_group = cfg.tokens, cfg.width, cfg.groups, cfg.per_group
    n, rows = cfg.devices, cfg.per_group * cfg.tokens
    pairs = max(1, (n - 1) // 2)
    kv_shape = pltpu.VMEM((2, tokens, width), F32)
    own = call(
        functools.partial(pack_kernel, cfg),
        (kv_shape,) * groups,
        far_off(key_vectors, value_vectors),
        [
            pltpu.VMEM(key_vectors.shape, F32),
            pltpu.VMEM(value_vectors.shape, F32),
            pltpu.SemaphoreType.DMA((2,)),
        ],
        [pl.BlockSpec(memory_space=pl.ANY)] * 2,
    )
    kv = []
    for g in range(groups):
        kv.append([own[g]])
        for k in range(1, n):
            kv[g].append(shifted(own[g], "ctx", k))

    prep_shapes = (
        pltpu.VMEM((rows, 3 * width), BF16),
        pltpu.VMEM((per_group * width, 3 * width), BF16),
        pltpu.VMEM((per_group, 2 * width, 2 * tokens), BF16),
        pltpu.VMEM((width, 2 * per_group * width), BF16),
        pltpu.VMEM((width, 2 * per_group * width), BF16),
        pltpu.VMEM((tokens, rows), F32),
        pltpu.VMEM((width, rows), F32),
        pltpu.VMEM((1, rows), F32),
        pltpu.VMEM((1, rows), F32),
    )
    prep = call(
        functools.partial(prep_kernel, cfg),
        tuple(shape for shape in prep_shapes for _ in range(groups)),
        far_off(queries, query_feature, key_feature) + near(*own),
        [
            pltpu.VMEM(queries.shape, F32),
            pltpu.VMEM(query_feature.shape, F32),
            pltpu.VMEM(key_feature.shape, F32),
            pltpu.SemaphoreType.DMA((3,)),
        ],
        [pl.BlockSpec(memory_space=pl.ANY)] * 3 + [VMEM] * groups,
    )
    attend_shapes = (
        pltpu.VMEM((2 * tokens, rows), F32),
        pltpu.VMEM((2, width, rows), BF16),
        pltpu.VMEM((1, rows), F32),
        pltpu.VMEM((per_group, 2 * width, tokens), F32),
    )
    scratch = [
        pltpu.VMEM((pairs, 2, 2 * tokens, width), F32),
        pltpu.VMEM((pairs, 2, 2 * tokens, width), F32),
        pltpu.VMEM((1, rows), F32),
        pltpu.VMEM((1, rows), F32),
        pltpu.VMEM((width, rows), F32),
        pltpu.VMEM((width, rows), F32),
        pltpu.VMEM((1, rows), F32),
        pltpu.VMEM((pairs, 2 * tokens, rows), F32),
        pltpu.VMEM((pairs, per_group, 2 * width, 2 * tokens), F32),
    ]
    for_query, mine = [], []
    for g in range(groups):
        q_3, wk_t, fq, wk_2, wq_2, *window = prep[g::groups]
        win, grad, gden, dfq, *grads = call(
            functools.partial(attend_kernel, cfg),
            attend_shapes + (kv_shape,) * (n - 2),
            near(q_3, wk_t, fq, wk_2, *window, *kv[g][1:]),
            scratch,
            megabytes=20,
        )
        soft, *near_grads = call(
            functools.partial(window_kernel, cfg),
            (pltpu.VMEM((2, 2 * tokens, rows), BF16), kv_shape, kv_shape),
            near(q_3, win, grad, gden, kv[g][0], kv[g][1]),
        )
        grads = near_grads + grads
        for_query.append((soft, dfq, fq, wq_2, kv[g][0], kv[g][1]))
        back = []
        for k in range(1, n):
            back.append(shifted(grads[k], "ctx", -k))
        mine.append(call(add_kernel, kv_shape, near(grads[0], *back)))
    query_grad = call(
        functools.partial(query_kernel, cfg),
        jax.ShapeDtypeStruct(queries.shape, F32),
        near(*[x for parts in zip(*for_query) for x in parts]),
    )
    other = [lax.ppermute(part, "sub", [(0, 1), (1, 0)]) for part in mine]
    key_grad, value_grad = call(
        functools.partial(place_kernel, cfg),
        (
            jax.ShapeDtypeStruct(key_vectors.shape, F32),
            jax.ShapeDtypeStruct(value_vectors.shape, F32),
        ),
        near(*mine, *other),
    )
    return query_grad, key_grad, value_grad


def solution(mesh):
    placed = (
        P(("groups", "ctx"), ("head", "sub"), None),
        P(("groups", "ctx"), "head", None),
        P(("groups", "ctx"), "head", None),
        P(("head", "sub"), None, None),
        P(("head", "sub"), None, None),
    )

    def step(queries, key_vectors, value_vectors, query_feature, key_feature):
        return jax.shard_map(
            layer,
            mesh=mesh,
            in_specs=placed,
            out_specs=placed[:3],
            check_vma=False,
        )(queries, key_vectors, value_vectors, query_feature, key_feature)

    return step
```

```python
import functools
import math

import jax
import jax.numpy as jnp
from jax import lax
from jax.experimental import pallas as pl
from jax.experimental.pallas import tpu as pltpu
from jax.sharding import PartitionSpec as P


NEG = -1e30
F32 = jnp.float32
BF16 = jnp.bfloat16

NT = (((1,), (1,)), ((), ()))
NN = (((1,), (0,)), ((), ()))


def along(value, pairs):
    return lax.ppermute(value, "ctx", pairs)


def split2(x):
    hi = x.astype(BF16)
    return hi, (x - hi.astype(F32)).astype(BF16)


def split3(x):
    hi = x.astype(BF16)
    rest = x - hi.astype(F32)
    mid = rest.astype(BF16)
    return hi, mid, (rest - mid.astype(F32)).astype(BF16)


def lanes(*parts):
    return jnp.concatenate(parts, axis=1)


def stack(*parts):
    return jnp.concatenate(parts, axis=0)


def dot(a, b, dims):
    return lax.dot_general(a, b, dims, preferred_element_type=F32)


def short3(a, b, dims):
    join = lanes if dims is NT else stack
    return dot(lanes(a[0], a[0], a[1]), join(b[0], b[1], b[0]), dims)


def short6(a, b, dims):
    join = lanes if dims is NT else stack
    return dot(
        lanes(a[1], a[2], a[0], a[1], a[0], a[0]),
        join(b[1], b[0], b[2], b[0], b[1], b[0]),
        dims,
    )


def tall3(a, b, dims):
    m = a[0].shape[0]
    both = dot(stack(a[0], a[1]), b[0], dims)
    return both[:m] + (both[m:] + dot(a[0], b[1], dims))


def wide3(a, b, dims):
    if dims is NT:
        n = b[0].shape[0]
        both = dot(a[0], stack(b[0], b[1]), dims)
    else:
        n = b[0].shape[1]
        both = dot(a[0], lanes(b[0], b[1]), dims)
    return both[:, :n] + (both[:, n:] + dot(a[1], b[0], dims))


def colsum(x):
    return jnp.sum(x, axis=0, keepdims=True)


def colmax(x):
    return jnp.max(x, axis=0, keepdims=True)


def softmax_pair(mapped):
    up = jnp.exp(mapped - colmax(mapped))
    low = jnp.exp(jnp.min(mapped, axis=0, keepdims=True) - mapped)
    return stack(up * (1.0 / colsum(up)), low * (1.0 / colsum(low)))


def softmax_pair_back(feat, grad, width):
    up, low = feat[:width], feat[width:]
    gup, glow = grad[:width], grad[width:]
    return up * (gup - colsum(up * gup)) - low * (glow - colsum(low * glow))


def pack_kernel(cfg, *refs):
    sources, kv_refs = refs[:5], refs[5 : 5 + cfg.groups]
    q_ref, wq_ref, wk_ref, up_ref, k_ref, v_ref, sems = refs[5 + cfg.groups :]
    copies = [
        pltpu.make_async_copy(src, dst, sems.at[i])
        for i, (src, dst) in enumerate(zip(sources, (k_ref, v_ref, q_ref, wq_ref, wk_ref)))
    ]
    for copy in copies:
        copy.start()
    sub = lax.axis_index("sub")
    for slot, ref in enumerate((k_ref, v_ref)):
        copies[slot].wait()
        for g, kv_ref in enumerate(kv_refs):
            value = ref[:, cfg.starts[0] + g, :]
            for s in range(1, len(cfg.starts)):
                value = jnp.where(sub == s, ref[:, cfg.starts[s] + g, :], value)
            kv_ref[slot] = value
            if g == 0:
                up_ref[slot] = value
    copies[2].wait()
    for h in range(cfg.per_group):
        up_ref[2 + h] = q_ref[:, h, :]
    for copy in copies[3:]:
        copy.wait()


def prep_kernel(cfg, g, moved, *refs):
    if moved:
        up_ref, wq_ref, *outs = refs

        @pl.when(lax.axis_index("ctx") == cfg.helper)
        def _():
            rows = [up_ref[2 + h] for h in range(cfg.per_group)]
            prepare_rows(cfg, g, rows, up_ref, wq_ref, outs)

        return
    q_ref, wq_ref, wk_ref, own_ref, *outs = refs
    width, per_group = cfg.width, cfg.per_group
    rows = [q_ref[:, g * per_group + h, :] for h in range(per_group)]
    prepare_rows(cfg, g, rows, own_ref, wq_ref, outs[:6])
    wk_out, wk2_out, wq2_out = outs[6:]
    for h in range(per_group):
        part = split3(wk_ref[g * per_group + h].T)
        for i in range(3):
            wk_out[h * width : (h + 1) * width, i * width : (i + 1) * width] = part[i]
        for out, ref in ((wk2_out, wk_ref), (wq2_out, wq_ref)):
            part = split2(ref[g * per_group + h])
            for i in range(2):
                at = i * per_group + h
                out[:, at * width : (at + 1) * width] = part[i]


def prepare_rows(cfg, g, blocks, own_ref, wq_ref, outs):
    tokens, width, per_group = cfg.tokens, cfg.width, cfg.per_group
    rows = per_group * tokens
    scale = 1.0 / math.sqrt(width)
    key_row = lax.broadcasted_iota(jnp.int32, (tokens, rows), 0)
    query_col = lax.broadcasted_iota(jnp.int32, (tokens, rows), 1) % tokens
    q_out, fq_out, a_out, num_out, top_out, mass_out = outs
    query = split3(stack(*blocks))
    for i in range(3):
        q_out[:, i * width : (i + 1) * width] = query[i]
    scores = short6(split3(own_ref[0]), query, NT) * scale
    scores = jnp.where(key_row <= query_col, scores, NEG)
    top = colmax(scores)
    a = jnp.exp(scores - top)
    a_out[...] = a
    top_out[...] = top
    mass_out[...] = colsum(a)
    num_out[...] = short3(split2(own_ref[1].T), split2(a), NN)
    for h in range(per_group):
        piece = tuple(x[h * tokens : (h + 1) * tokens] for x in query)
        feat = split2(softmax_pair(short6(split3(wq_ref[g * per_group + h].T), piece, NT)))
        fq_out[h, :, :tokens] = feat[0]
        fq_out[h, :, tokens:] = feat[1]


def position_of(cfg, kind):
    here = lax.axis_index("ctx")
    if kind == "stay":
        return jnp.where(here == cfg.devices - 1, -1, here)
    if kind == "moved":
        return jnp.where(here == cfg.helper, cfg.devices - 1, -1)
    return here


def guarded(kernel):
    def body(cfg, kind, n, grads_at, *refs):
        here = position_of(cfg, kind)
        if kind == "all":
            kernel(cfg, n, here, *refs)
            return

        @pl.when(here >= 0)
        def _():
            kernel(cfg, n, here, *refs)

        @pl.when(here < 0)
        def _():
            for ref in refs[grads_at[0] : grads_at[1]]:
                ref[...] = jnp.zeros(ref.shape, F32)

    return body


@guarded
def attend_kernel(cfg, n, here, *refs):
    q_ref, fq_ref, a_ref, num_ref, top_ref, mass_ref, wk_t_ref, wk2_ref = refs[:8]
    kv_in = (None,) + refs[8 : 7 + n]
    win_ref, grad_ref, gden_ref, dfq_s = refs[7 + n : 11 + n]
    kv_out = (None, None) + refs[11 + n : 9 + 2 * n]
    (kv_s, dkv_s, top_s, mass_s, tnum_s, num_s, den_s, c_s, fk_s) = refs[9 + 2 * n :]
    tokens, width, per_group = cfg.tokens, cfg.width, cfg.per_group
    scale = 1.0 / math.sqrt(width)

    for k in range(2, n):
        pair, at = k // 2 - 1, (k % 2) * tokens
        for slot in range(2):
            kv_s[pair, slot, at : at + tokens, :] = kv_in[k][slot]
    query = tuple(q_ref[:, i * width : (i + 1) * width] for i in range(3))

    def head(x, h):
        return x[:, h * tokens : (h + 1) * tokens]

    def fq(h):
        return fq_ref[h, :, :tokens], fq_ref[h, :, tokens:]

    key_prev, value_prev = kv_in[1][0], kv_in[1][1]
    s_prev = short6(split3(key_prev), query, NT) * scale
    s_prev = jnp.where(here > 0, s_prev, NEG)
    top = jnp.maximum(top_ref[...], colmax(s_prev))
    a_prev = jnp.exp(s_prev - top)
    fade = jnp.exp(top_ref[...] - top)
    a_own = a_ref[...] * fade
    win_ref[:tokens] = a_own
    win_ref[tokens:] = a_prev
    mass = mass_ref[...] * fade + colsum(a_prev)
    wnum = num_ref[...] * fade + short3(
        split2(value_prev.T), split2(a_prev), NN
    )
    top_s[...] = top
    mass_s[...] = mass
    tnum_s[...] = wnum
    num_s[...] = wnum
    den_s[...] = mass

    def far_forward(pair, blocks):
        keys = blocks * tokens
        key, value = kv_s[pair, 0, :keys], kv_s[pair, 1, :keys]
        key_3 = split3(key)
        s = short6(key_3, query, NT) * scale
        old = top_s[...]
        new = jnp.maximum(old, colmax(s))
        p = jnp.exp(s - new)
        factor = jnp.exp(old - new)
        top_s[...] = new
        mass_s[...] = mass_s[...] * factor + colsum(p)
        wk_t = tuple(wk_t_ref[:, i * width : (i + 1) * width] for i in range(3))
        mapped = short6(wk_t, key_3, NT)
        for h in range(per_group):
            feat_t = softmax_pair(mapped[h * width : (h + 1) * width])
            fk_s[pair, h, :, :keys] = feat_t
            c_s[pair, :keys, h * tokens : (h + 1) * tokens] = wide3(
                split2(feat_t.T), fq(h), NN
            )
        c = c_s[pair, :keys]
        den_s[...] += colsum(c)
        value_t = split2(value.T)
        tnum_s[...] = tnum_s[...] * factor + tall3(value_t, split2(p), NN)
        num_s[...] += tall3(value_t, split2(c), NN)

    count = jnp.maximum(here - 1, 0)

    def over_far(body):
        def step(pair, carry):
            body(pair, 2)
            return carry

        if n > 3:
            lax.fori_loop(0, count // 2, step, 0)

        @pl.when(count % 2 == 1)
        def _():
            body(count // 2, 1)

    over_far(far_forward)

    inv = 1.0 / den_s[...]
    out = num_s[...] * inv
    residual = out - tnum_s[...] * (1.0 / mass_s[...])
    grad = residual * inv
    grad_2 = split2(grad)
    grad_ref[0] = grad_2[0]
    grad_ref[1] = grad_2[1]
    grad_den = -colsum(residual * out) * inv
    gden_ref[...] = grad_den
    dfq_s[...] = jnp.zeros_like(dfq_s)

    def far_backward(pair, blocks):
        keys = blocks * tokens
        dc = short3(split2(kv_s[pair, 1, :keys]), grad_2, NN) + grad_den
        dc_2 = split2(dc)
        dkv_s[pair, 1, :keys] = wide3(split2(c_s[pair, :keys]), grad_2, NT)
        pieces = []
        for h in range(per_group):
            feat_t = fk_s[pair, h, :, :keys]
            dc_h = tuple(head(x, h) for x in dc_2)
            dfq_s[h] += wide3(split2(feat_t), dc_h, NN)
            dfk = short3(fq(h), dc_h, NT)
            pieces.append(softmax_pair_back(feat_t, dfk, width))
        wk_2 = wk2_ref[:, : per_group * width], wk2_ref[:, per_group * width :]
        dkv_s[pair, 0, :keys] = tall3(wk_2, split2(stack(*pieces)), NN).T

    over_far(far_backward)
    for k in range(2, n):
        pair, at = k // 2 - 1, (k % 2) * tokens

        @pl.when(here >= k)
        def _():
            for slot in range(2):
                kv_out[k][slot] = dkv_s[pair, slot, at : at + tokens, :]

        @pl.when(here < k)
        def _():
            kv_out[k][...] = jnp.zeros((2, tokens, width), F32)


@guarded
def window_kernel(cfg, n, here, *refs):
    q_ref, win_ref, grad_ref, gden_ref, own_ref, prev_ref, soft_ref = refs[:7]
    outs = refs[7:]
    tokens, width = cfg.tokens, cfg.width
    scale = 1.0 / math.sqrt(width)
    grad_2 = grad_ref[0], grad_ref[1]
    win = win_ref[...]
    soft = short3(split2(stack(own_ref[1], prev_ref[1])), grad_2, NN) + gden_ref[...]
    soft_2 = split2(win * soft * scale)
    soft_ref[0] = soft_2[0]
    soft_ref[1] = soft_2[1]
    dk = wide3(soft_2, (q_ref[:, :width], q_ref[:, width : 2 * width]), NN)
    dv = wide3(split2(win), grad_2, NT)
    for k, out in enumerate(outs):
        out[0] = dk[k * tokens : (k + 1) * tokens]
        out[1] = dv[k * tokens : (k + 1) * tokens]


def query_rows(cfg, soft_ref, dfq_ref, fq_ref, wq2_ref, own_ref, prev_ref):
    tokens, width, per_group = cfg.tokens, cfg.width, cfg.per_group
    key_t = split2(stack(own_ref[0], prev_ref[0]).T)
    dq = tall3(key_t, (soft_ref[0], soft_ref[1]), NN)
    for h in range(per_group):
        feat = fq_ref[h, :, :tokens].astype(F32) + fq_ref[h, :, tokens:].astype(F32)
        back = softmax_pair_back(feat, dfq_ref[h], width)
        wq_2 = tuple(
            wq2_ref[:, (i * per_group + h) * width : (i * per_group + h + 1) * width]
            for i in range(2)
        )
        dq_h = dq[:, h * tokens : (h + 1) * tokens] + short3(wq_2, split2(back), NN)
        yield h, dq_h.T


def query_kernel(cfg, *refs):
    dq_ref = refs[-1]
    for g in range(cfg.groups):
        if cfg.moves and g == 0:
            here = lax.axis_index("ctx")

            @pl.when(here != cfg.devices - 1)
            def _():
                for h, value in query_rows(cfg, *refs[:6]):
                    dq_ref[:, h, :] = value

            @pl.when(here == cfg.devices - 1)
            def _():
                for h in range(cfg.per_group):
                    dq_ref[:, h, :] = refs[-2][2 + h]
        else:
            for h, value in query_rows(cfg, *refs[6 * g : 6 * g + 6]):
                dq_ref[:, g * cfg.per_group + h, :] = value


def moved_query_kernel(cfg, *refs):
    own_grad_ref, out_ref = refs[6], refs[7]

    @pl.when(lax.axis_index("ctx") == cfg.helper)
    def _():
        out_ref[:2] = own_grad_ref[...]
        for h, value in query_rows(cfg, *refs[:6]):
            out_ref[2 + h] = value

    @pl.when(lax.axis_index("ctx") != cfg.helper)
    def _():
        out_ref[...] = jnp.zeros(out_ref.shape, F32)


def add_kernel(*refs):
    total = refs[0][...]
    for ref in refs[1:-1]:
        total = total + ref[:2]
    refs[-1][...] = total


def place_kernel(cfg, *refs):
    sub = lax.axis_index("sub")
    mine, other = refs[: cfg.groups], refs[cfg.groups : 2 * cfg.groups]
    for slot, ref in enumerate(refs[2 * cfg.groups :]):
        for g in range(cfg.groups_dev):
            if cfg.shared:
                ref[:, g, :] = mine[g][slot] + other[g][slot]
            else:
                owner, at = g // cfg.groups, g % cfg.groups
                ref[:, g, :] = jnp.where(sub == owner, mine[at][slot], other[at][slot])


class Config:
    def __init__(self, queries, key_vectors):
        self.tokens, self.heads, self.width = queries.shape
        self.groups_dev = key_vectors.shape[1]
        self.devices = lax.axis_size("ctx")
        subs = lax.axis_size("sub")
        assert subs == 2
        size = self.heads * subs // self.groups_dev
        self.shared = self.heads < size
        self.groups = max(1, self.heads // size)
        self.per_group = self.heads // self.groups
        self.starts = [s * self.heads // size for s in range(subs)]
        if self.shared:
            assert self.groups_dev == 1
        assert self.devices % 2 == 0
        self.moves = self.devices == 4 and self.groups == 2
        self.helper = self.devices - 3


VMEM = pl.BlockSpec(memory_space=pltpu.VMEM)


def limit(mebibytes):
    return pltpu.CompilerParams(vmem_limit_bytes=mebibytes << 20)


def near(*arrays):
    return [pltpu.with_memory_space_constraint(x, pltpu.VMEM) for x in arrays]


def far_off(*arrays):
    return [pltpu.with_memory_space_constraint(x, pltpu.HBM) for x in arrays]


def call(kernel, outs, args, scratch=(), ins=None, megabytes=16):
    return pl.pallas_call(
        kernel,
        out_shape=outs,
        in_specs=ins or [VMEM] * len(args),
        out_specs=jax.tree.map(lambda _: VMEM, outs),
        scratch_shapes=scratch,
        compiler_params=limit(megabytes),
    )(*args)


def layer(queries, key_vectors, value_vectors, query_feature, key_feature):
    cfg = Config(queries, key_vectors)
    tokens, width, groups, per_group = cfg.tokens, cfg.width, cfg.groups, cfg.per_group
    n, rows = cfg.devices, cfg.per_group * cfg.tokens
    kv_shape = pltpu.VMEM((2, tokens, width), F32)
    up_shape = pltpu.VMEM((2 + per_group, tokens, width), F32)
    loaded = (queries, query_feature, key_feature)
    *own, q, wq, wk, up = call(
        functools.partial(pack_kernel, cfg),
        (kv_shape,) * groups + tuple(pltpu.VMEM(x.shape, F32) for x in loaded) + (up_shape,),
        far_off(key_vectors, value_vectors, *loaded),
        [
            pltpu.VMEM(key_vectors.shape, F32),
            pltpu.VMEM(value_vectors.shape, F32),
            pltpu.SemaphoreType.DMA((5,)),
        ],
        [pl.BlockSpec(memory_space=pl.ANY)] * 5,
    )

    row_shapes = (
        pltpu.VMEM((rows, 3 * width), BF16),
        pltpu.VMEM((per_group, 2 * width, 2 * tokens), BF16),
        pltpu.VMEM((tokens, rows), F32),
        pltpu.VMEM((width, rows), F32),
        pltpu.VMEM((1, rows), F32),
        pltpu.VMEM((1, rows), F32),
    )
    weight_shapes = (
        pltpu.VMEM((per_group * width, 3 * width), BF16),
        pltpu.VMEM((width, 2 * per_group * width), BF16),
        pltpu.VMEM((width, 2 * per_group * width), BF16),
    )
    attend_shapes = (
        pltpu.VMEM((2 * tokens, rows), F32),
        pltpu.VMEM((2, width, rows), BF16),
        pltpu.VMEM((1, rows), F32),
        pltpu.VMEM((per_group, 2 * width, tokens), F32),
    )
    soft_shape = pltpu.VMEM((2, 2 * tokens, rows), BF16)

    def task(kind, ready, weights, kv):
        count = len(kv)
        pairs = max(1, (count - 1) // 2)
        wk_t, wk_2, wq_2 = weights
        scratch = [
            pltpu.VMEM((pairs, 2, 2 * tokens, width), F32),
            pltpu.VMEM((pairs, 2, 2 * tokens, width), F32),
            pltpu.VMEM((1, rows), F32),
            pltpu.VMEM((1, rows), F32),
            pltpu.VMEM((width, rows), F32),
            pltpu.VMEM((width, rows), F32),
            pltpu.VMEM((1, rows), F32),
            pltpu.VMEM((pairs, 2 * tokens, rows), F32),
            pltpu.VMEM((pairs, per_group, 2 * width, 2 * tokens), F32),
        ]
        win, grad, gden, dfq, *grads = call(
            functools.partial(
                attend_kernel, cfg, kind, count, (11 + count, 9 + 2 * count)
            ),
            attend_shapes + (kv_shape,) * (count - 2),
            near(*ready, wk_t, wk_2, *kv[1:]),
            scratch,
            megabytes=20,
        )
        soft, *near_grads = call(
            functools.partial(window_kernel, cfg, kind, count, (7, 9)),
            (soft_shape, kv_shape, kv_shape),
            near(ready[0], win, grad, gden, kv[0], kv[1]),
        )
        return near_grads + grads, (soft, dfq, ready[1], wq_2, kv[0], kv[1])

    def add(*parts):
        return call(add_kernel, kv_shape, near(*parts))

    def down(k, limit=n):
        return [(i, i + k) for i in range(limit - k)]

    def back(k, limit=n):
        return [(i, i - k) for i in range(k, limit)]

    ready, weights, kv, moved_kv = [], [], [], None
    for g in range(groups):
        limit = n - 1 if cfg.moves and g == 0 else n
        kv.append([own[g]])
        for k in range(1, limit):
            kv[g].append(along(own[g], down(k, limit)))
        made = call(
            functools.partial(prep_kernel, cfg, g, False),
            row_shapes + weight_shapes,
            near(q, wq, wk, own[g]),
        )
        ready.append(made[:6])
        weights.append(made[6:])
    if cfg.moves:
        arrived = along(up, [(n - 1, cfg.helper)])
        above = along(own[0], [(n - 2, cfg.helper)])
        moved_ready = call(
            functools.partial(prep_kernel, cfg, 0, True), row_shapes, near(arrived, wq)
        )
        moved_kv = [arrived, above, kv[0][0], kv[0][1]]

    for_query, mine, extra = [], [], []
    for g in range(groups):
        stays = cfg.moves and g == 0
        grads, query_parts = task(
            "stay" if stays else "all", ready[g], weights[g], kv[g]
        )
        for_query.append(query_parts)
        if not stays:
            got = [along(grads[k], back(k)) for k in range(1, n)]
            mine.append(add(grads[0], *got))
            continue
        moved, moved_parts = task("moved", moved_ready, weights[0], moved_kv)
        answer = call(
            functools.partial(moved_query_kernel, cfg),
            up_shape,
            near(*moved_parts, moved[0]),
        )
        first = add(grads[1], moved[3])
        got = [
            along(grads[2], back(2, n - 1)),
            along(grads[1], [(n - 2, n - 3)]),
            along(first, [(cfg.helper, 0)]),
            along(moved[1], [(cfg.helper, n - 2)]),
            along(answer, [(cfg.helper, n - 1)]),
        ]
        extra = [got[-1]]
        mine.append(add(grads[0], moved[2], *got))
    query_grad = call(
        functools.partial(query_kernel, cfg),
        jax.ShapeDtypeStruct(queries.shape, F32),
        near(*[x for parts in for_query for x in parts], *extra),
    )
    other = [lax.ppermute(part, "sub", [(0, 1), (1, 0)]) for part in mine]
    key_grad, value_grad = call(
        functools.partial(place_kernel, cfg),
        (
            jax.ShapeDtypeStruct(key_vectors.shape, F32),
            jax.ShapeDtypeStruct(value_vectors.shape, F32),
        ),
        near(*mine, *other),
    )
    return query_grad, key_grad, value_grad


def solution(mesh):
    placed = (
        P(("groups", "ctx"), ("head", "sub"), None),
        P(("groups", "ctx"), "head", None),
        P(("groups", "ctx"), "head", None),
        P(("head", "sub"), None, None),
        P(("head", "sub"), None, None),
    )

    def step(queries, key_vectors, value_vectors, query_feature, key_feature):
        return jax.shard_map(
            layer,
            mesh=mesh,
            in_specs=placed,
            out_specs=placed[:3],
            check_vma=False,
        )(queries, key_vectors, value_vectors, query_feature, key_feature)

    return step
```

```python
import functools
import math

import jax
import jax.numpy as jnp
from jax import lax
from jax.experimental import pallas as pl
from jax.experimental.pallas import tpu as pltpu
from jax.sharding import PartitionSpec as P


NEG = -1e30
F32 = jnp.float32
BF16 = jnp.bfloat16

NT = (((1,), (1,)), ((), ()))
NN = (((1,), (0,)), ((), ()))


def along(value, pairs):
    return lax.ppermute(value, "ctx", pairs)


def split2(x):
    hi = x.astype(BF16)
    return hi, (x - hi.astype(F32)).astype(BF16)


def split3(x):
    hi = x.astype(BF16)
    rest = x - hi.astype(F32)
    mid = rest.astype(BF16)
    return hi, mid, (rest - mid.astype(F32)).astype(BF16)


def lanes(*parts):
    return jnp.concatenate(parts, axis=1)


def stack(*parts):
    return jnp.concatenate(parts, axis=0)


def dot(a, b, dims):
    return lax.dot_general(a, b, dims, preferred_element_type=F32)


def short3(a, b, dims):
    join = lanes if dims is NT else stack
    return dot(lanes(a[0], a[0], a[1]), join(b[0], b[1], b[0]), dims)


def short6(a, b, dims):
    join = lanes if dims is NT else stack
    return dot(
        lanes(a[1], a[2], a[0], a[1], a[0], a[0]),
        join(b[1], b[0], b[2], b[0], b[1], b[0]),
        dims,
    )


def tall3(a, b, dims):
    m = a[0].shape[0]
    both = dot(stack(a[0], a[1]), b[0], dims)
    return both[:m] + (both[m:] + dot(a[0], b[1], dims))


def wide3(a, b, dims):
    if dims is NT:
        n = b[0].shape[0]
        both = dot(a[0], stack(b[0], b[1]), dims)
    else:
        n = b[0].shape[1]
        both = dot(a[0], lanes(b[0], b[1]), dims)
    return both[:, :n] + (both[:, n:] + dot(a[1], b[0], dims))


def colsum(x):
    return jnp.sum(x, axis=0, keepdims=True)


def colmax(x):
    return jnp.max(x, axis=0, keepdims=True)


def softmax_pair(mapped):
    up = jnp.exp(mapped - colmax(mapped))
    low = jnp.exp(jnp.min(mapped, axis=0, keepdims=True) - mapped)
    return stack(up * (1.0 / colsum(up)), low * (1.0 / colsum(low)))


def softmax_pair_back(feat, grad, width):
    up, low = feat[:width], feat[width:]
    gup, glow = grad[:width], grad[width:]
    return up * (gup - colsum(up * gup)) - low * (glow - colsum(low * glow))


def pack_kernel(cfg, *refs):
    sources, kv_refs = refs[:5], refs[5 : 5 + cfg.groups]
    q_ref, wq_ref, wk_ref, up_ref, k_ref, v_ref, sems = refs[5 + cfg.groups :]
    copies = [
        pltpu.make_async_copy(src, dst, sems.at[i])
        for i, (src, dst) in enumerate(zip(sources, (k_ref, v_ref, q_ref, wq_ref, wk_ref)))
    ]
    for copy in copies:
        copy.start()
    sub = lax.axis_index("sub")
    for slot, ref in enumerate((k_ref, v_ref)):
        copies[slot].wait()
        for g, kv_ref in enumerate(kv_refs):
            value = ref[:, cfg.starts[0] + g, :]
            for s in range(1, len(cfg.starts)):
                value = jnp.where(sub == s, ref[:, cfg.starts[s] + g, :], value)
            kv_ref[slot] = value
            if g == 0:
                up_ref[slot] = value
    copies[2].wait()
    for h in range(cfg.per_group):
        up_ref[2 + h] = q_ref[:, h, :]
    for copy in copies[3:]:
        copy.wait()


def prep_kernel(cfg, g, moved, *refs):
    if moved:
        up_ref, wq_ref, *outs = refs

        @pl.when(lax.axis_index("ctx") == cfg.helper)
        def _():
            rows = [up_ref[2 + h] for h in range(cfg.per_group)]
            prepare_rows(cfg, g, rows, up_ref, wq_ref, outs)

        return
    q_ref, wq_ref, wk_ref, own_ref, *outs = refs
    width, per_group = cfg.width, cfg.per_group
    rows = [q_ref[:, g * per_group + h, :] for h in range(per_group)]
    prepare_rows(cfg, g, rows, own_ref, wq_ref, outs[:6])
    wk_out, wk2_out, wq2_out = outs[6:]
    for h in range(per_group):
        part = split3(wk_ref[g * per_group + h].T)
        for i in range(3):
            wk_out[h * width : (h + 1) * width, i * width : (i + 1) * width] = part[i]
        for out, ref in ((wk2_out, wk_ref), (wq2_out, wq_ref)):
            part = split2(ref[g * per_group + h])
            for i in range(2):
                at = i * per_group + h
                out[:, at * width : (at + 1) * width] = part[i]


def prepare_rows(cfg, g, blocks, own_ref, wq_ref, outs):
    tokens, width, per_group = cfg.tokens, cfg.width, cfg.per_group
    rows = per_group * tokens
    scale = 1.0 / math.sqrt(width)
    key_row = lax.broadcasted_iota(jnp.int32, (tokens, rows), 0)
    query_col = lax.broadcasted_iota(jnp.int32, (tokens, rows), 1) % tokens
    q_out, fq_out, a_out, num_out, top_out, mass_out = outs
    query = split3(stack(*blocks))
    for i in range(3):
        q_out[:, i * width : (i + 1) * width] = query[i]
    scores = short6(split3(own_ref[0]), query, NT) * scale
    scores = jnp.where(key_row <= query_col, scores, NEG)
    top = colmax(scores)
    a = jnp.exp(scores - top)
    a_out[...] = a
    top_out[...] = top
    mass_out[...] = colsum(a)
    num_out[...] = short3(split2(own_ref[1].T), split2(a), NN)
    for h in range(per_group):
        piece = tuple(x[h * tokens : (h + 1) * tokens] for x in query)
        feat = split2(softmax_pair(short6(split3(wq_ref[g * per_group + h].T), piece, NT)))
        fq_out[h, :, :tokens] = feat[0]
        fq_out[h, :, tokens:] = feat[1]


def position_of(cfg, kind):
    here = lax.axis_index("ctx")
    if kind == "stay":
        return jnp.where(here == cfg.devices - 1, -1, here)
    if kind == "moved":
        return jnp.where(here == cfg.helper, cfg.devices - 1, -1)
    return here


def guarded(kernel):
    def body(cfg, kind, n, grads_at, *refs):
        here = position_of(cfg, kind)
        if kind == "all":
            kernel(cfg, n, here, *refs)
            return

        @pl.when(here >= 0)
        def _():
            kernel(cfg, n, here, *refs)

        @pl.when(here < 0)
        def _():
            for ref in refs[grads_at[0] : grads_at[1]]:
                ref[...] = jnp.zeros(ref.shape, F32)

    return body


@guarded
def attend_kernel(cfg, n, here, *refs):
    q_ref, fq_ref, a_ref, num_ref, top_ref, mass_ref, wk_t_ref, wk2_ref = refs[:8]
    kv_in = (None,) + refs[8 : 7 + n]
    win_ref, grad_ref, gden_ref, dfq_s = refs[7 + n : 11 + n]
    kv_out = (None, None) + refs[11 + n : 9 + 2 * n]
    (kv_s, dkv_s, top_s, mass_s, tnum_s, num_s, den_s, c_s, fk_s) = refs[9 + 2 * n :]
    tokens, width, per_group = cfg.tokens, cfg.width, cfg.per_group
    scale = 1.0 / math.sqrt(width)

    for k in range(2, n):
        pair, at = k // 2 - 1, (k % 2) * tokens
        for slot in range(2):
            kv_s[pair, slot, at : at + tokens, :] = kv_in[k][slot]
    query = tuple(q_ref[:, i * width : (i + 1) * width] for i in range(3))

    def head(x, h):
        return x[:, h * tokens : (h + 1) * tokens]

    def fq(h):
        return fq_ref[h, :, :tokens], fq_ref[h, :, tokens:]

    key_prev, value_prev = kv_in[1][0], kv_in[1][1]
    s_prev = short6(split3(key_prev), query, NT) * scale
    s_prev = jnp.where(here > 0, s_prev, NEG)
    top = jnp.maximum(top_ref[...], colmax(s_prev))
    a_prev = jnp.exp(s_prev - top)
    fade = jnp.exp(top_ref[...] - top)
    a_own = a_ref[...] * fade
    win_ref[:tokens] = a_own
    win_ref[tokens:] = a_prev
    mass = mass_ref[...] * fade + colsum(a_prev)
    wnum = num_ref[...] * fade + short3(
        split2(value_prev.T), split2(a_prev), NN
    )
    top_s[...] = top
    mass_s[...] = mass
    tnum_s[...] = wnum
    num_s[...] = wnum
    den_s[...] = mass

    def far_forward(pair, blocks):
        keys = blocks * tokens
        key, value = kv_s[pair, 0, :keys], kv_s[pair, 1, :keys]
        key_3 = split3(key)
        s = short6(key_3, query, NT) * scale
        old = top_s[...]
        new = jnp.maximum(old, colmax(s))
        p = jnp.exp(s - new)
        factor = jnp.exp(old - new)
        top_s[...] = new
        mass_s[...] = mass_s[...] * factor + colsum(p)
        wk_t = tuple(wk_t_ref[:, i * width : (i + 1) * width] for i in range(3))
        mapped = short6(wk_t, key_3, NT)
        for h in range(per_group):
            feat_t = softmax_pair(mapped[h * width : (h + 1) * width])
            fk_s[pair, h, :, :keys] = feat_t
            c_s[pair, :keys, h * tokens : (h + 1) * tokens] = wide3(
                split2(feat_t.T), fq(h), NN
            )
        c = c_s[pair, :keys]
        den_s[...] += colsum(c)
        value_t = split2(value.T)
        tnum_s[...] = tnum_s[...] * factor + tall3(value_t, split2(p), NN)
        num_s[...] += tall3(value_t, split2(c), NN)

    count = jnp.maximum(here - 1, 0)

    def over_far(body):
        def step(pair, carry):
            body(pair, 2)
            return carry

        if n > 3:
            lax.fori_loop(0, count // 2, step, 0)

        @pl.when(count % 2 == 1)
        def _():
            body(count // 2, 1)

    over_far(far_forward)

    inv = 1.0 / den_s[...]
    out = num_s[...] * inv
    residual = out - tnum_s[...] * (1.0 / mass_s[...])
    grad = residual * inv
    grad_2 = split2(grad)
    grad_ref[0] = grad_2[0]
    grad_ref[1] = grad_2[1]
    grad_den = -colsum(residual * out) * inv
    gden_ref[...] = grad_den
    dfq_s[...] = jnp.zeros_like(dfq_s)

    def far_backward(pair, blocks):
        keys = blocks * tokens
        dc = short3(split2(kv_s[pair, 1, :keys]), grad_2, NN) + grad_den
        dc_2 = split2(dc)
        dkv_s[pair, 1, :keys] = wide3(split2(c_s[pair, :keys]), grad_2, NT)
        pieces = []
        for h in range(per_group):
            feat_t = fk_s[pair, h, :, :keys]
            dc_h = tuple(head(x, h) for x in dc_2)
            dfq_s[h] += wide3(split2(feat_t), dc_h, NN)
            dfk = short3(fq(h), dc_h, NT)
            pieces.append(softmax_pair_back(feat_t, dfk, width))
        wk_2 = wk2_ref[:, : per_group * width], wk2_ref[:, per_group * width :]
        dkv_s[pair, 0, :keys] = tall3(wk_2, split2(stack(*pieces)), NN).T

    over_far(far_backward)
    for k in range(2, n):
        pair, at = k // 2 - 1, (k % 2) * tokens

        @pl.when(here >= k)
        def _():
            for slot in range(2):
                kv_out[k][slot] = dkv_s[pair, slot, at : at + tokens, :]

        @pl.when(here < k)
        def _():
            kv_out[k][...] = jnp.zeros((2, tokens, width), F32)


@guarded
def window_kernel(cfg, n, here, *refs):
    q_ref, win_ref, grad_ref, gden_ref, own_ref, prev_ref, soft_ref = refs[:7]
    outs = refs[7:]
    tokens, width = cfg.tokens, cfg.width
    scale = 1.0 / math.sqrt(width)
    grad_2 = grad_ref[0], grad_ref[1]
    win = win_ref[...]
    soft = short3(split2(stack(own_ref[1], prev_ref[1])), grad_2, NN) + gden_ref[...]
    soft_2 = split2(win * soft * scale)
    soft_ref[0] = soft_2[0]
    soft_ref[1] = soft_2[1]
    dk = wide3(soft_2, (q_ref[:, :width], q_ref[:, width : 2 * width]), NN)
    dv = wide3(split2(win), grad_2, NT)
    for k, out in enumerate(outs):
        out[0] = dk[k * tokens : (k + 1) * tokens]
        out[1] = dv[k * tokens : (k + 1) * tokens]


def query_rows(cfg, soft_ref, dfq_ref, fq_ref, wq2_ref, own_ref, prev_ref):
    tokens, width, per_group = cfg.tokens, cfg.width, cfg.per_group
    key_t = split2(stack(own_ref[0], prev_ref[0]).T)
    dq = tall3(key_t, (soft_ref[0], soft_ref[1]), NN)
    for h in range(per_group):
        feat = fq_ref[h, :, :tokens].astype(F32) + fq_ref[h, :, tokens:].astype(F32)
        back = softmax_pair_back(feat, dfq_ref[h], width)
        wq_2 = tuple(
            wq2_ref[:, (i * per_group + h) * width : (i * per_group + h + 1) * width]
            for i in range(2)
        )
        dq_h = dq[:, h * tokens : (h + 1) * tokens] + short3(wq_2, split2(back), NN)
        yield h, dq_h.T


def query_kernel(cfg, *refs):
    dq_ref = refs[-1]
    for g in range(cfg.groups):
        if cfg.moves and g == 0:
            here = lax.axis_index("ctx")

            @pl.when(here != cfg.devices - 1)
            def _():
                for h, value in query_rows(cfg, *refs[:6]):
                    dq_ref[:, h, :] = value

            @pl.when(here == cfg.devices - 1)
            def _():
                for h in range(cfg.per_group):
                    dq_ref[:, h, :] = refs[-2][2 + h]
        else:
            for h, value in query_rows(cfg, *refs[6 * g : 6 * g + 6]):
                dq_ref[:, g * cfg.per_group + h, :] = value


def moved_query_kernel(cfg, *refs):
    own_grad_ref, out_ref = refs[6], refs[7]

    @pl.when(lax.axis_index("ctx") == cfg.helper)
    def _():
        out_ref[:2] = own_grad_ref[...]
        for h, value in query_rows(cfg, *refs[:6]):
            out_ref[2 + h] = value

    @pl.when(lax.axis_index("ctx") != cfg.helper)
    def _():
        out_ref[...] = jnp.zeros(out_ref.shape, F32)


def add_kernel(*refs):
    total = refs[0][...]
    for ref in refs[1:-1]:
        total = total + ref[:2]
    refs[-1][...] = total


def place_kernel(cfg, *refs):
    sub = lax.axis_index("sub")
    mine, other = refs[: cfg.groups], refs[cfg.groups : 2 * cfg.groups]
    for slot, ref in enumerate(refs[2 * cfg.groups :]):
        for g in range(cfg.groups_dev):
            if cfg.shared:
                ref[:, g, :] = mine[g][slot] + other[g][slot]
            else:
                owner, at = g // cfg.groups, g % cfg.groups
                ref[:, g, :] = jnp.where(sub == owner, mine[at][slot], other[at][slot])


class Config:
    def __init__(self, queries, key_vectors):
        self.tokens, self.heads, self.width = queries.shape
        self.groups_dev = key_vectors.shape[1]
        self.devices = lax.axis_size("ctx")
        subs = lax.axis_size("sub")
        assert subs == 2
        size = self.heads * subs // self.groups_dev
        self.shared = self.heads < size
        self.groups = max(1, self.heads // size)
        self.per_group = self.heads // self.groups
        self.starts = [s * self.heads // size for s in range(subs)]
        if self.shared:
            assert self.groups_dev == 1
        assert self.devices % 2 == 0
        self.moves = self.devices == 4 and self.groups == 2
        self.helper = self.devices - 3


VMEM = pl.BlockSpec(memory_space=pltpu.VMEM)


def limit(mebibytes):
    return pltpu.CompilerParams(vmem_limit_bytes=mebibytes << 20)


def near(*arrays):
    return [pltpu.with_memory_space_constraint(x, pltpu.VMEM) for x in arrays]


def far_off(*arrays):
    return [pltpu.with_memory_space_constraint(x, pltpu.HBM) for x in arrays]


def call(kernel, outs, args, scratch=(), ins=None, megabytes=16):
    return pl.pallas_call(
        kernel,
        out_shape=outs,
        in_specs=ins or [VMEM] * len(args),
        out_specs=jax.tree.map(lambda _: VMEM, outs),
        scratch_shapes=scratch,
        compiler_params=limit(megabytes),
    )(*args)


def layer(queries, key_vectors, value_vectors, query_feature, key_feature):
    cfg = Config(queries, key_vectors)
    tokens, width, groups, per_group = cfg.tokens, cfg.width, cfg.groups, cfg.per_group
    n, rows = cfg.devices, cfg.per_group * cfg.tokens
    kv_shape = pltpu.VMEM((2, tokens, width), F32)
    up_shape = pltpu.VMEM((2 + per_group, tokens, width), F32)
    loaded = (queries, query_feature, key_feature)
    *own, q, wq, wk, up = call(
        functools.partial(pack_kernel, cfg),
        (kv_shape,) * groups + tuple(pltpu.VMEM(x.shape, F32) for x in loaded) + (up_shape,),
        far_off(key_vectors, value_vectors, *loaded),
        [
            pltpu.VMEM(key_vectors.shape, F32),
            pltpu.VMEM(value_vectors.shape, F32),
            pltpu.SemaphoreType.DMA((5,)),
        ],
        [pl.BlockSpec(memory_space=pl.ANY)] * 5,
    )

    row_shapes = (
        pltpu.VMEM((rows, 3 * width), BF16),
        pltpu.VMEM((per_group, 2 * width, 2 * tokens), BF16),
        pltpu.VMEM((tokens, rows), F32),
        pltpu.VMEM((width, rows), F32),
        pltpu.VMEM((1, rows), F32),
        pltpu.VMEM((1, rows), F32),
    )
    weight_shapes = (
        pltpu.VMEM((per_group * width, 3 * width), BF16),
        pltpu.VMEM((width, 2 * per_group * width), BF16),
        pltpu.VMEM((width, 2 * per_group * width), BF16),
    )
    attend_shapes = (
        pltpu.VMEM((2 * tokens, rows), F32),
        pltpu.VMEM((2, width, rows), BF16),
        pltpu.VMEM((1, rows), F32),
        pltpu.VMEM((per_group, 2 * width, tokens), F32),
    )
    soft_shape = pltpu.VMEM((2, 2 * tokens, rows), BF16)

    def task(kind, ready, weights, kv):
        count = len(kv)
        pairs = max(1, (count - 1) // 2)
        wk_t, wk_2, wq_2 = weights
        scratch = [
            pltpu.VMEM((pairs, 2, 2 * tokens, width), F32),
            pltpu.VMEM((pairs, 2, 2 * tokens, width), F32),
            pltpu.VMEM((1, rows), F32),
            pltpu.VMEM((1, rows), F32),
            pltpu.VMEM((width, rows), F32),
            pltpu.VMEM((width, rows), F32),
            pltpu.VMEM((1, rows), F32),
            pltpu.VMEM((pairs, 2 * tokens, rows), F32),
            pltpu.VMEM((pairs, per_group, 2 * width, 2 * tokens), F32),
        ]
        win, grad, gden, dfq, *grads = call(
            functools.partial(
                attend_kernel, cfg, kind, count, (11 + count, 9 + 2 * count)
            ),
            attend_shapes + (kv_shape,) * (count - 2),
            near(*ready, wk_t, wk_2, *kv[1:]),
            scratch,
            megabytes=20,
        )
        soft, *near_grads = call(
            functools.partial(window_kernel, cfg, kind, count, (7, 9)),
            (soft_shape, kv_shape, kv_shape),
            near(ready[0], win, grad, gden, kv[0], kv[1]),
        )
        return near_grads + grads, (soft, dfq, ready[1], wq_2, kv[0], kv[1])

    def add(*parts):
        return call(add_kernel, kv_shape, near(*parts))

    def down(k, limit=n):
        return [(i, i + k) for i in range(limit - k)]

    def back(k, limit=n):
        return [(i, i - k) for i in range(k, limit)]

    ready, weights, kv, moved_kv = [], [], [], None
    for g in range(groups):
        limit = n - 1 if cfg.moves and g == 0 else n
        kv.append([own[g]])
        for k in range(1, limit):
            kv[g].append(along(own[g], down(k, limit)))
        made = call(
            functools.partial(prep_kernel, cfg, g, False),
            row_shapes + weight_shapes,
            near(q, wq, wk, own[g]),
        )
        ready.append(made[:6])
        weights.append(made[6:])
    if cfg.moves:
        arrived = along(up, [(n - 1, cfg.helper)])
        above = along(own[0], [(n - 2, cfg.helper)])
        moved_ready = call(
            functools.partial(prep_kernel, cfg, 0, True), row_shapes, near(arrived, wq)
        )
        moved_kv = [arrived, above, kv[0][0], kv[0][1]]

    for_query, mine, extra = [], [], []
    for g in range(groups):
        stays = cfg.moves and g == 0
        grads, query_parts = task(
            "stay" if stays else "all", ready[g], weights[g], kv[g]
        )
        for_query.append(query_parts)
        if not stays:
            got = []
            for k in range(1, n):
                routes = [back(k)]
                if cfg.moves and k == 2:
                    routes = [[pair] for pair in back(k)]
                for route in routes:
                    got.append(along(grads[k], route))
            mine.append(add(grads[0], *got))
            continue
        moved, moved_parts = task("moved", moved_ready, weights[0], moved_kv)
        answer = call(
            functools.partial(moved_query_kernel, cfg),
            up_shape,
            near(*moved_parts, moved[0]),
        )
        first = add(grads[1], moved[3])
        got = [
            along(grads[2], back(2, n - 1)),
            along(grads[1], [(n - 2, n - 3)]),
            along(first, [(cfg.helper, 0)]),
            along(moved[1], [(cfg.helper, n - 2)]),
            along(answer, [(cfg.helper, n - 1)]),
        ]
        extra = [got[-1]]
        mine.append(add(grads[0], moved[2], *got))
    query_grad = call(
        functools.partial(query_kernel, cfg),
        jax.ShapeDtypeStruct(queries.shape, F32),
        near(*[x for parts in for_query for x in parts], *extra),
    )
    other = [lax.ppermute(part, "sub", [(0, 1), (1, 0)]) for part in mine]
    key_grad, value_grad = call(
        functools.partial(place_kernel, cfg),
        (
            jax.ShapeDtypeStruct(key_vectors.shape, F32),
            jax.ShapeDtypeStruct(value_vectors.shape, F32),
        ),
        near(*mine, *other),
    )
    return query_grad, key_grad, value_grad


def solution(mesh):
    placed = (
        P(("groups", "ctx"), ("head", "sub"), None),
        P(("groups", "ctx"), "head", None),
        P(("groups", "ctx"), "head", None),
        P(("head", "sub"), None, None),
        P(("head", "sub"), None, None),
    )

    def step(queries, key_vectors, value_vectors, query_feature, key_feature):
        return jax.shard_map(
            layer,
            mesh=mesh,
            in_specs=placed,
            out_specs=placed[:3],
            check_vma=False,
        )(queries, key_vectors, value_vectors, query_feature, key_feature)

    return step
```

```python
import functools
import math

import jax
import jax.numpy as jnp
from jax import lax
from jax.experimental import pallas as pl
from jax.experimental.pallas import tpu as pltpu
from jax.sharding import PartitionSpec as P


NEG = -1e30
F32 = jnp.float32
BF16 = jnp.bfloat16

NT = (((1,), (1,)), ((), ()))
NN = (((1,), (0,)), ((), ()))


def along(value, pairs):
    return lax.ppermute(value, "ctx", pairs)


def split2(x):
    hi = x.astype(BF16)
    return hi, (x - hi.astype(F32)).astype(BF16)


def split3(x):
    hi = x.astype(BF16)
    rest = x - hi.astype(F32)
    mid = rest.astype(BF16)
    return hi, mid, (rest - mid.astype(F32)).astype(BF16)


def lanes(*parts):
    return jnp.concatenate(parts, axis=1)


def stack(*parts):
    return jnp.concatenate(parts, axis=0)


def dot(a, b, dims):
    return lax.dot_general(a, b, dims, preferred_element_type=F32)


def short3(a, b, dims):
    join = lanes if dims is NT else stack
    return dot(lanes(a[0], a[0], a[1]), join(b[0], b[1], b[0]), dims)


def short6(a, b, dims):
    join = lanes if dims is NT else stack
    return dot(
        lanes(a[1], a[2], a[0], a[1], a[0], a[0]),
        join(b[1], b[0], b[2], b[0], b[1], b[0]),
        dims,
    )


def tall3(a, b, dims):
    m = a[0].shape[0]
    both = dot(stack(a[0], a[1]), b[0], dims)
    return both[:m] + (both[m:] + dot(a[0], b[1], dims))


def wide3(a, b, dims):
    if dims is NT:
        n = b[0].shape[0]
        both = dot(a[0], stack(b[0], b[1]), dims)
    else:
        n = b[0].shape[1]
        both = dot(a[0], lanes(b[0], b[1]), dims)
    return both[:, :n] + (both[:, n:] + dot(a[1], b[0], dims))


def colsum(x):
    return jnp.sum(x, axis=0, keepdims=True)


def colmax(x):
    return jnp.max(x, axis=0, keepdims=True)


def softmax_pair(mapped):
    up = jnp.exp(mapped - colmax(mapped))
    low = jnp.exp(jnp.min(mapped, axis=0, keepdims=True) - mapped)
    return stack(up * (1.0 / colsum(up)), low * (1.0 / colsum(low)))


def softmax_pair_back(feat, grad, width):
    up, low = feat[:width], feat[width:]
    gup, glow = grad[:width], grad[width:]
    return up * (gup - colsum(up * gup)) - low * (glow - colsum(low * glow))


def pack_kernel(cfg, *refs):
    sources, kv_refs = refs[:5], refs[5 : 5 + cfg.groups]
    q_ref, wq_ref, wk_ref, up_ref, k_ref, v_ref, sems = refs[5 + cfg.groups :]
    copies = [
        pltpu.make_async_copy(src, dst, sems.at[i])
        for i, (src, dst) in enumerate(zip(sources, (k_ref, v_ref, q_ref, wq_ref, wk_ref)))
    ]
    for copy in copies:
        copy.start()
    sub = lax.axis_index("sub")
    for slot, ref in enumerate((k_ref, v_ref)):
        copies[slot].wait()
        for g, kv_ref in enumerate(kv_refs):
            value = ref[:, cfg.starts[0] + g, :]
            for s in range(1, len(cfg.starts)):
                value = jnp.where(sub == s, ref[:, cfg.starts[s] + g, :], value)
            kv_ref[slot] = value
            if g == 0:
                up_ref[slot] = value
    copies[2].wait()
    for h in range(cfg.per_group):
        up_ref[2 + h] = q_ref[:, h, :]
    for copy in copies[3:]:
        copy.wait()


def prep_kernel(cfg, g, moved, *refs):
    if moved:
        up_ref, wq_ref, *outs = refs

        @pl.when(lax.axis_index("ctx") == cfg.helper)
        def _():
            rows = [up_ref[2 + h] for h in range(cfg.per_group)]
            prepare_rows(cfg, g, rows, up_ref, wq_ref, outs)

        return
    q_ref, wq_ref, wk_ref, own_ref, *outs = refs
    width, per_group = cfg.width, cfg.per_group
    rows = [q_ref[:, g * per_group + h, :] for h in range(per_group)]
    prepare_rows(cfg, g, rows, own_ref, wq_ref, outs[:6])
    wk_out, wk2_out, wq2_out = outs[6:]
    for h in range(per_group):
        part = split3(wk_ref[g * per_group + h].T)
        for i in range(3):
            wk_out[h * width : (h + 1) * width, i * width : (i + 1) * width] = part[i]
        for out, ref in ((wk2_out, wk_ref), (wq2_out, wq_ref)):
            part = split2(ref[g * per_group + h])
            for i in range(2):
                at = i * per_group + h
                out[:, at * width : (at + 1) * width] = part[i]


def prepare_rows(cfg, g, blocks, own_ref, wq_ref, outs):
    tokens, width, per_group = cfg.tokens, cfg.width, cfg.per_group
    rows = per_group * tokens
    scale = 1.0 / math.sqrt(width)
    key_row = lax.broadcasted_iota(jnp.int32, (tokens, rows), 0)
    query_col = lax.broadcasted_iota(jnp.int32, (tokens, rows), 1) % tokens
    q_out, fq_out, a_out, num_out, top_out, mass_out = outs
    query = split3(stack(*blocks))
    for i in range(3):
        q_out[:, i * width : (i + 1) * width] = query[i]
    scores = short6(split3(own_ref[0]), query, NT) * scale
    scores = jnp.where(key_row <= query_col, scores, NEG)
    top = colmax(scores)
    a = jnp.exp(scores - top)
    a_out[...] = a
    top_out[...] = top
    mass_out[...] = colsum(a)
    num_out[...] = short3(split2(own_ref[1].T), split2(a), NN)
    for h in range(per_group):
        piece = tuple(x[h * tokens : (h + 1) * tokens] for x in query)
        feat = split2(softmax_pair(short6(split3(wq_ref[g * per_group + h].T), piece, NT)))
        fq_out[h, :, :tokens] = feat[0]
        fq_out[h, :, tokens:] = feat[1]


def position_of(cfg, kind):
    here = lax.axis_index("ctx")
    if kind == "stay":
        return jnp.where(here == cfg.devices - 1, -1, here)
    if kind == "moved":
        return jnp.where(here == cfg.helper, cfg.devices - 1, -1)
    return here


def guarded(kernel):
    def body(cfg, kind, n, grads_at, *refs):
        here = position_of(cfg, kind)
        if kind == "all":
            kernel(cfg, kind, n, here, *refs)
            return

        @pl.when(here >= 0)
        def _():
            kernel(cfg, kind, n, here, *refs)

        @pl.when(here < 0)
        def _():
            for ref in refs[grads_at[0] : grads_at[1]]:
                ref[...] = jnp.zeros(ref.shape, F32)

    return body


@guarded
def attend_kernel(cfg, kind, n, here, *refs):
    if n > 4:
        attend_rows(cfg, n, here, None, *refs)
    elif kind == "moved":
        attend_rows(cfg, n, here, n - 2, *refs)
    else:
        for far in range(n - 1):

            @pl.when(jnp.maximum(here - 1, 0) == far)
            def _():
                attend_rows(cfg, n, here, far, *refs)


def attend_rows(cfg, n, here, far, *refs):
    q_ref, fq_ref, a_ref, num_ref, top_ref, mass_ref, wk_t_ref, wk2_ref = refs[:8]
    kv_in = (None,) + refs[8 : 7 + n]
    win_ref, grad_ref, gden_ref, dfq_s = refs[7 + n : 11 + n]
    kv_out = (None, None) + refs[11 + n : 9 + 2 * n]
    (kv_s, dkv_s, top_s, mass_s, tnum_s, num_s, den_s, c_s, fk_s) = refs[9 + 2 * n :]
    tokens, width, per_group = cfg.tokens, cfg.width, cfg.per_group
    scale = 1.0 / math.sqrt(width)

    for k in range(2, n):
        pair, at = k // 2 - 1, (k % 2) * tokens
        for slot in range(2):
            kv_s[pair, slot, at : at + tokens, :] = kv_in[k][slot]
    query = tuple(q_ref[:, i * width : (i + 1) * width] for i in range(3))

    def head(x, h):
        return x[:, h * tokens : (h + 1) * tokens]

    def fq(h):
        return fq_ref[h, :, :tokens], fq_ref[h, :, tokens:]

    key_prev, value_prev = kv_in[1][0], kv_in[1][1]
    s_prev = short6(split3(key_prev), query, NT) * scale
    s_prev = jnp.where(here > 0, s_prev, NEG)
    top = jnp.maximum(top_ref[...], colmax(s_prev))
    a_prev = jnp.exp(s_prev - top)
    fade = jnp.exp(top_ref[...] - top)
    a_own = a_ref[...] * fade
    win_ref[:tokens] = a_own
    win_ref[tokens:] = a_prev
    mass = mass_ref[...] * fade + colsum(a_prev)
    wnum = num_ref[...] * fade + short3(
        split2(value_prev.T), split2(a_prev), NN
    )
    top_s[...] = top
    mass_s[...] = mass
    tnum_s[...] = wnum
    num_s[...] = wnum
    den_s[...] = mass

    def far_forward(pair, blocks):
        keys = blocks * tokens
        key, value = kv_s[pair, 0, :keys], kv_s[pair, 1, :keys]
        key_3 = split3(key)
        s = short6(key_3, query, NT) * scale
        old = top_s[...]
        new = jnp.maximum(old, colmax(s))
        p = jnp.exp(s - new)
        factor = jnp.exp(old - new)
        top_s[...] = new
        mass_s[...] = mass_s[...] * factor + colsum(p)
        wk_t = tuple(wk_t_ref[:, i * width : (i + 1) * width] for i in range(3))
        mapped = short6(wk_t, key_3, NT)
        for h in range(per_group):
            feat_t = softmax_pair(mapped[h * width : (h + 1) * width])
            fk_s[pair, h, :, :keys] = feat_t
            c_s[pair, :keys, h * tokens : (h + 1) * tokens] = wide3(
                split2(feat_t.T), fq(h), NN
            )
        c = c_s[pair, :keys]
        den_s[...] += colsum(c)
        value_t = split2(value.T)
        tnum_s[...] = tnum_s[...] * factor + tall3(value_t, split2(p), NN)
        num_s[...] += tall3(value_t, split2(c), NN)

    count = jnp.maximum(here - 1, 0)

    def over_far(body):
        def step(pair, carry):
            body(pair, 2)
            return carry

        if far is not None:
            for first in range(0, far, 2):
                body(first // 2, min(2, far - first))
            return
        lax.fori_loop(0, count // 2, step, 0)

        @pl.when(count % 2 == 1)
        def _():
            body(count // 2, 1)

    over_far(far_forward)

    inv = 1.0 / den_s[...]
    out = num_s[...] * inv
    residual = out - tnum_s[...] * (1.0 / mass_s[...])
    grad = residual * inv
    grad_2 = split2(grad)
    grad_ref[0] = grad_2[0]
    grad_ref[1] = grad_2[1]
    grad_den = -colsum(residual * out) * inv
    gden_ref[...] = grad_den
    dfq_s[...] = jnp.zeros_like(dfq_s)

    def far_backward(pair, blocks):
        keys = blocks * tokens
        dc = short3(split2(kv_s[pair, 1, :keys]), grad_2, NN) + grad_den
        dc_2 = split2(dc)
        dkv_s[pair, 1, :keys] = wide3(split2(c_s[pair, :keys]), grad_2, NT)
        pieces = []
        for h in range(per_group):
            feat_t = fk_s[pair, h, :, :keys]
            dc_h = tuple(head(x, h) for x in dc_2)
            dfq_s[h] += wide3(split2(feat_t), dc_h, NN)
            dfk = short3(fq(h), dc_h, NT)
            pieces.append(softmax_pair_back(feat_t, dfk, width))
        wk_2 = wk2_ref[:, : per_group * width], wk2_ref[:, per_group * width :]
        dkv_s[pair, 0, :keys] = tall3(wk_2, split2(stack(*pieces)), NN).T

    over_far(far_backward)
    for k in range(2, n):
        pair, at = k // 2 - 1, (k % 2) * tokens
        if far is not None:
            if k - 2 < far:
                for slot in range(2):
                    kv_out[k][slot] = dkv_s[pair, slot, at : at + tokens, :]
            else:
                kv_out[k][...] = jnp.zeros((2, tokens, width), F32)
            continue

        @pl.when(here >= k)
        def _():
            for slot in range(2):
                kv_out[k][slot] = dkv_s[pair, slot, at : at + tokens, :]

        @pl.when(here < k)
        def _():
            kv_out[k][...] = jnp.zeros((2, tokens, width), F32)


@guarded
def window_kernel(cfg, kind, n, here, *refs):
    q_ref, win_ref, grad_ref, gden_ref, own_ref, prev_ref, soft_ref = refs[:7]
    outs = refs[7:]
    tokens, width = cfg.tokens, cfg.width
    scale = 1.0 / math.sqrt(width)
    grad_2 = grad_ref[0], grad_ref[1]
    win = win_ref[...]
    soft = short3(split2(stack(own_ref[1], prev_ref[1])), grad_2, NN) + gden_ref[...]
    soft_2 = split2(win * soft * scale)
    soft_ref[0] = soft_2[0]
    soft_ref[1] = soft_2[1]
    dk = wide3(soft_2, (q_ref[:, :width], q_ref[:, width : 2 * width]), NN)
    dv = wide3(split2(win), grad_2, NT)
    for k, out in enumerate(outs):
        out[0] = dk[k * tokens : (k + 1) * tokens]
        out[1] = dv[k * tokens : (k + 1) * tokens]


def query_rows(cfg, soft_ref, dfq_ref, fq_ref, wq2_ref, own_ref, prev_ref):
    tokens, width, per_group = cfg.tokens, cfg.width, cfg.per_group
    key_t = split2(stack(own_ref[0], prev_ref[0]).T)
    dq = tall3(key_t, (soft_ref[0], soft_ref[1]), NN)
    for h in range(per_group):
        feat = fq_ref[h, :, :tokens].astype(F32) + fq_ref[h, :, tokens:].astype(F32)
        back = softmax_pair_back(feat, dfq_ref[h], width)
        wq_2 = tuple(
            wq2_ref[:, (i * per_group + h) * width : (i * per_group + h + 1) * width]
            for i in range(2)
        )
        dq_h = dq[:, h * tokens : (h + 1) * tokens] + short3(wq_2, split2(back), NN)
        yield h, dq_h.T


def query_kernel(cfg, *refs):
    dq_ref = refs[-1]
    for g in range(cfg.groups):
        if cfg.moves and g == 0:
            here = lax.axis_index("ctx")

            @pl.when(here != cfg.devices - 1)
            def _():
                for h, value in query_rows(cfg, *refs[:6]):
                    dq_ref[:, h, :] = value

            @pl.when(here == cfg.devices - 1)
            def _():
                for h in range(cfg.per_group):
                    dq_ref[:, h, :] = refs[-2][2 + h]
        else:
            for h, value in query_rows(cfg, *refs[6 * g : 6 * g + 6]):
                dq_ref[:, g * cfg.per_group + h, :] = value


def moved_query_kernel(cfg, *refs):
    own_grad_ref, out_ref = refs[6], refs[7]

    @pl.when(lax.axis_index("ctx") == cfg.helper)
    def _():
        out_ref[:2] = own_grad_ref[...]
        for h, value in query_rows(cfg, *refs[:6]):
            out_ref[2 + h] = value

    @pl.when(lax.axis_index("ctx") != cfg.helper)
    def _():
        out_ref[...] = jnp.zeros(out_ref.shape, F32)


def add_kernel(*refs):
    total = refs[0][...]
    for ref in refs[1:-1]:
        total = total + ref[:2]
    refs[-1][...] = total


def place_kernel(cfg, *refs):
    sub = lax.axis_index("sub")
    mine, other = refs[: cfg.groups], refs[cfg.groups : 2 * cfg.groups]
    for slot, ref in enumerate(refs[2 * cfg.groups :]):
        for g in range(cfg.groups_dev):
            if cfg.shared:
                ref[:, g, :] = mine[g][slot] + other[g][slot]
            else:
                owner, at = g // cfg.groups, g % cfg.groups
                ref[:, g, :] = jnp.where(sub == owner, mine[at][slot], other[at][slot])


class Config:
    def __init__(self, queries, key_vectors):
        self.tokens, self.heads, self.width = queries.shape
        self.groups_dev = key_vectors.shape[1]
        self.devices = lax.axis_size("ctx")
        subs = lax.axis_size("sub")
        assert subs == 2
        size = self.heads * subs // self.groups_dev
        self.shared = self.heads < size
        self.groups = max(1, self.heads // size)
        self.per_group = self.heads // self.groups
        self.starts = [s * self.heads // size for s in range(subs)]
        if self.shared:
            assert self.groups_dev == 1
        assert self.devices % 2 == 0
        self.moves = self.devices == 4 and self.groups == 2
        self.helper = self.devices - 3


VMEM = pl.BlockSpec(memory_space=pltpu.VMEM)


def limit(mebibytes):
    return pltpu.CompilerParams(vmem_limit_bytes=mebibytes << 20)


def near(*arrays):
    return [pltpu.with_memory_space_constraint(x, pltpu.VMEM) for x in arrays]


def far_off(*arrays):
    return [pltpu.with_memory_space_constraint(x, pltpu.HBM) for x in arrays]


def call(kernel, outs, args, scratch=(), ins=None, megabytes=16):
    return pl.pallas_call(
        kernel,
        out_shape=outs,
        in_specs=ins or [VMEM] * len(args),
        out_specs=jax.tree.map(lambda _: VMEM, outs),
        scratch_shapes=scratch,
        compiler_params=limit(megabytes),
    )(*args)


def layer(queries, key_vectors, value_vectors, query_feature, key_feature):
    cfg = Config(queries, key_vectors)
    tokens, width, groups, per_group = cfg.tokens, cfg.width, cfg.groups, cfg.per_group
    n, rows = cfg.devices, cfg.per_group * cfg.tokens
    kv_shape = pltpu.VMEM((2, tokens, width), F32)
    up_shape = pltpu.VMEM((2 + per_group, tokens, width), F32)
    loaded = (queries, query_feature, key_feature)
    *own, q, wq, wk, up = call(
        functools.partial(pack_kernel, cfg),
        (kv_shape,) * groups + tuple(pltpu.VMEM(x.shape, F32) for x in loaded) + (up_shape,),
        far_off(key_vectors, value_vectors, *loaded),
        [
            pltpu.VMEM(key_vectors.shape, F32),
            pltpu.VMEM(value_vectors.shape, F32),
            pltpu.SemaphoreType.DMA((5,)),
        ],
        [pl.BlockSpec(memory_space=pl.ANY)] * 5,
    )

    row_shapes = (
        pltpu.VMEM((rows, 3 * width), BF16),
        pltpu.VMEM((per_group, 2 * width, 2 * tokens), BF16),
        pltpu.VMEM((tokens, rows), F32),
        pltpu.VMEM((width, rows), F32),
        pltpu.VMEM((1, rows), F32),
        pltpu.VMEM((1, rows), F32),
    )
    weight_shapes = (
        pltpu.VMEM((per_group * width, 3 * width), BF16),
        pltpu.VMEM((width, 2 * per_group * width), BF16),
        pltpu.VMEM((width, 2 * per_group * width), BF16),
    )
    attend_shapes = (
        pltpu.VMEM((2 * tokens, rows), F32),
        pltpu.VMEM((2, width, rows), BF16),
        pltpu.VMEM((1, rows), F32),
        pltpu.VMEM((per_group, 2 * width, tokens), F32),
    )
    soft_shape = pltpu.VMEM((2, 2 * tokens, rows), BF16)

    def task(kind, ready, weights, kv):
        count = len(kv)
        pairs = max(1, (count - 1) // 2)
        wk_t, wk_2, wq_2 = weights
        scratch = [
            pltpu.VMEM((pairs, 2, 2 * tokens, width), F32),
            pltpu.VMEM((pairs, 2, 2 * tokens, width), F32),
            pltpu.VMEM((1, rows), F32),
            pltpu.VMEM((1, rows), F32),
            pltpu.VMEM((width, rows), F32),
            pltpu.VMEM((width, rows), F32),
            pltpu.VMEM((1, rows), F32),
            pltpu.VMEM((pairs, 2 * tokens, rows), F32),
            pltpu.VMEM((pairs, per_group, 2 * width, 2 * tokens), F32),
        ]
        win, grad, gden, dfq, *grads = call(
            functools.partial(
                attend_kernel, cfg, kind, count, (11 + count, 9 + 2 * count)
            ),
            attend_shapes + (kv_shape,) * (count - 2),
            near(*ready, wk_t, wk_2, *kv[1:]),
            scratch,
            megabytes=20,
        )
        soft, *near_grads = call(
            functools.partial(window_kernel, cfg, kind, count, (7, 9)),
            (soft_shape, kv_shape, kv_shape),
            near(ready[0], win, grad, gden, kv[0], kv[1]),
        )
        return near_grads + grads, (soft, dfq, ready[1], wq_2, kv[0], kv[1])

    def add(*parts):
        return call(add_kernel, kv_shape, near(*parts))

    def down(k, limit=n):
        return [(i, i + k) for i in range(limit - k)]

    def back(k, limit=n):
        return [(i, i - k) for i in range(k, limit)]

    ready, weights, kv, moved_kv = [], [], [], None
    for g in range(groups):
        limit = n - 1 if cfg.moves and g == 0 else n
        kv.append([own[g]])
        for k in range(1, limit):
            kv[g].append(along(own[g], down(k, limit)))
        made = call(
            functools.partial(prep_kernel, cfg, g, False),
            row_shapes + weight_shapes,
            near(q, wq, wk, own[g]),
        )
        ready.append(made[:6])
        weights.append(made[6:])
    if cfg.moves:
        arrived = along(up, [(n - 1, cfg.helper)])
        above = along(own[0], [(n - 2, cfg.helper)])
        moved_ready = call(
            functools.partial(prep_kernel, cfg, 0, True), row_shapes, near(arrived, wq)
        )
        moved_kv = [arrived, above, kv[0][0], kv[0][1]]

    for_query, mine, extra = [], [], []
    for g in range(groups):
        stays = cfg.moves and g == 0
        grads, query_parts = task(
            "stay" if stays else "all", ready[g], weights[g], kv[g]
        )
        for_query.append(query_parts)
        if not stays:
            got = []
            for k in range(1, n):
                routes = [back(k)]
                if cfg.moves and k == 2:
                    routes = [[pair] for pair in back(k)]
                for route in routes:
                    got.append(along(grads[k], route))
            mine.append(add(grads[0], *got))
            continue
        moved, moved_parts = task("moved", moved_ready, weights[0], moved_kv)
        answer = call(
            functools.partial(moved_query_kernel, cfg),
            up_shape,
            near(*moved_parts, moved[0]),
        )
        first = add(grads[1], moved[3])
        got = [
            along(grads[2], back(2, n - 1)),
            along(grads[1], [(n - 2, n - 3)]),
            along(first, [(cfg.helper, 0)]),
            along(moved[1], [(cfg.helper, n - 2)]),
            along(answer, [(cfg.helper, n - 1)]),
        ]
        extra = [got[-1]]
        mine.append(add(grads[0], moved[2], *got))
    query_grad = call(
        functools.partial(query_kernel, cfg),
        jax.ShapeDtypeStruct(queries.shape, F32),
        near(*[x for parts in for_query for x in parts], *extra),
    )
    other = [lax.ppermute(part, "sub", [(0, 1), (1, 0)]) for part in mine]
    key_grad, value_grad = call(
        functools.partial(place_kernel, cfg),
        (
            jax.ShapeDtypeStruct(key_vectors.shape, F32),
            jax.ShapeDtypeStruct(value_vectors.shape, F32),
        ),
        near(*mine, *other),
    )
    return query_grad, key_grad, value_grad


def solution(mesh):
    placed = (
        P(("groups", "ctx"), ("head", "sub"), None),
        P(("groups", "ctx"), "head", None),
        P(("groups", "ctx"), "head", None),
        P(("head", "sub"), None, None),
        P(("head", "sub"), None, None),
    )

    def step(queries, key_vectors, value_vectors, query_feature, key_feature):
        return jax.shard_map(
            layer,
            mesh=mesh,
            in_specs=placed,
            out_specs=placed[:3],
            check_vma=False,
        )(queries, key_vectors, value_vectors, query_feature, key_feature)

    return step
```
